32 devices in a mesh: seq: 8 (over z, x), head: 2 (over y), enc: 2 (over core).
Axes of the slice: x: 2, y: 2, z: 4, core: 2. Of those that a mesh axis runs over, the one named last changes fastest.
Arguments:
- queries: bfloat16 [2560, 1024], P('seq', ('head', 'enc')), may hold values from -2000 to 2000
- keys: bfloat16 [2560, 1024], P('seq', ('head', 'enc')), may hold values from -2000 to 2000
- values: bfloat16 [2560, 1024], P('seq', ('head', 'enc')), may hold values from -6 to 6
- out_weight: bfloat16 [1024, 5120], P(('head', 'enc'), 'seq'), may hold values from -0.25 to 0.25
- q_gain: float32 [1024], P(('head', 'enc')), may hold values from 0.75 to 3
- k_gain: float32 [1024], P(('head', 'enc')), may hold values from 0.75 to 3
- gate: float32 [5120], P(('head', 'enc')), may hold values from 1 to 8
- valid_count: int32 [1], replicated, may hold values from 1280 to 2560
Outputs:
- update: bfloat16 [2560, 5120], P('seq', ('head', 'enc'))
The draws below stay inside these ranges and needn't reach their ends.
Inputs may be any that keep to these rules, and one draw needn't show every extreme that they name: Key positions from valid_count[0] on are padding and take no weight.
All inputs are finite; a program needn't handle non-finite values.
Results may differ from the reference program's by a relative error of at most 0.015.
The reference program's roundings to bfloat16 on the way count: a program that leaves them out, or rounds other values in their place, can miss the bound.
Values may be sent and summed in bfloat16 or wider, within the bound.
A program may use at most 64 MiB of HBM per device.

```python
import math
import jax
import jax.numpy as jnp
from jax import lax

D = 5120
HEAD_DIM = 128
GROUPS = 4
HEADS = 8
FEATURES = 1024
SEQ_LEN = 2560


def joint_draw(key):
    folded = jax.random.fold_in(key, 4111)
    subkeys = jax.random.split(folded, 5)
    column_head = jnp.arange(FEATURES) // HEAD_DIM
    rising = 1.0 + 2.0 * column_head.astype(jnp.float32) / max(HEADS - 1, 1)
    column_scale = rising * jnp.exp(jax.random.uniform(subkeys[0], (FEATURES,), minval=0.0, maxval=jnp.log(3.0)))
    row_query = jnp.exp(jax.random.uniform(subkeys[1], (SEQ_LEN, 1), minval=0.0, maxval=jnp.log(10.0)))
    row_key = jnp.exp(jax.random.uniform(subkeys[2], (SEQ_LEN, 1), minval=0.0, maxval=jnp.log(10.0)))
    query_draw = jax.random.normal(subkeys[3], (SEQ_LEN, FEATURES)) * row_query * column_scale[None, :]
    key_draw = jax.random.normal(subkeys[4], (SEQ_LEN, FEATURES)) * row_key * column_scale[None, :]
    query_draw = jnp.clip(query_draw, -2000.0, 2000.0)
    key_draw = jnp.clip(key_draw, -2000.0, 2000.0)
    return (query_draw.astype(jnp.bfloat16), key_draw.astype(jnp.bfloat16))


def draw_queries(key, part):
    return joint_draw(key)[0]


def draw_keys(key, part):
    return joint_draw(key)[1]


def spiked(drawn, stream_key, source, target, parts, factor):
    owner, partner = [(jnp.arange(drawn.shape[position]) // (drawn.shape[position] // parts)).reshape([-1 if axis == position else 1 for axis in range(drawn.ndim)]) for position in (source, target)]
    chosen = jax.random.permutation(stream_key, parts)[partner]
    strong = (owner == chosen) | (owner == (partner + parts // 2) % parts)
    return jnp.where(strong, factor * drawn, drawn)


def steps_of(key, shape, cuts, smallest, top_value):
    gain, own = 1.0, jax.random.fold_in(key, 6)
    for position, parts in cuts:
        heights = jnp.exp(jax.random.uniform(jax.random.fold_in(own, position), (parts,), jnp.float32, smallest / len(cuts), top_value / len(cuts)))
        gain = gain * jnp.repeat(heights, shape[position] // parts).reshape([-1 if axis == position else 1 for axis in range(len(shape))])
    return gain


def normal_values(stream_key, dims, scale, most, pieces=(), kind=jnp.bfloat16):
    result = scale * jax.random.normal(stream_key, dims, jnp.float32)
    if pieces:
        result = result * steps_of(stream_key, dims, pieces, -0.22, 0.18)
    return jnp.clip(result, -most, most).astype(kind)


def bell_draw_with(stream_key, extent, width, bound, pieces, heavy, kind=jnp.bfloat16):
    drawn = width * jax.random.normal(stream_key, extent, jnp.float32)
    if pieces:
        drawn = drawn * steps_of(stream_key, extent, pieces, -0.22, 0.18)
    return jnp.clip(spiked(drawn, jax.random.fold_in(stream_key, 3), *heavy), -bound, bound).astype(kind)


def setup_inputs(seed: int = 0) -> dict:
    key_list = jax.random.split(jax.random.key(seed), 9)
    queries = draw_queries(jax.random.fold_in(key_list[8], 71), 0)
    keys = draw_keys(jax.random.fold_in(key_list[8], 71), 0)
    values = normal_values(key_list[2], (SEQ_LEN, FEATURES), 1.0, 6.0, ((0, 8), (1, 4)))
    out_weight = bell_draw_with(key_list[3], (FEATURES, D), FEATURES ** -0.5, 0.25, ((0, 4), (1, 8)), (0, 1, 8, 2.0))
    q_gain = jnp.clip(jnp.exp(math.log(3.0) - 1.3862944 * jax.random.uniform(key_list[4], (FEATURES,), jnp.float32) ** steps_of(key_list[4], (FEATURES,), ((0, 4),), -0.2, 0.2)), 0.75, 3.0)
    k_gain = jnp.clip(jnp.exp(math.log(3.0) - 1.3862944 * jax.random.uniform(key_list[5], (FEATURES,), jnp.float32) ** steps_of(key_list[5], (FEATURES,), ((0, 4),), -0.2, 0.2)), 0.75, 3.0)
    gate = jnp.clip(jnp.exp(math.log(8.0) - 2.0794415 * jax.random.uniform(key_list[6], (D,), jnp.float32) ** steps_of(key_list[6], (D,), ((0, 4),), -0.2, 0.2)), 1.0, 8.0)
    valid_count = jax.random.randint(key_list[7], (1,), SEQ_LEN // 2, SEQ_LEN + 1).astype(jnp.int32)
    return {"queries": queries, "keys": keys, "values": values, "out_weight": out_weight, "q_gain": q_gain, "k_gain": k_gain, "gate": gate, "valid_count": valid_count}


epsilon = 1e-06

def normalize(matrix, gain_row):
    values32 = matrix.astype(jnp.float32)
    mean_square = lax.optimization_barrier(jnp.mean(values32 * values32, axis=1, keepdims=True))
    return (values32 * lax.rsqrt(mean_square + epsilon) * gain_row[None, :]).astype(jnp.bfloat16)

def reference(queries, keys, values, out_weight, q_gain, k_gain, gate, valid_count):
    query_norm = normalize(queries, q_gain)
    key_norm = normalize(keys, k_gain)
    key_limit = valid_count[0]
    usable = jnp.arange(SEQ_LEN, dtype=jnp.int32) < key_limit
    score_scale = HEAD_DIM ** (-0.5)
    block_size = 512 if SEQ_LEN % 512 == 0 else SEQ_LEN

    def split_heads(matrix):
        return matrix.reshape(SEQ_LEN, HEADS, HEAD_DIM).transpose(1, 0, 2)

    def attend_head(triple):
        query_head, key_head, value_head = triple
        query_blocks = query_head.reshape(SEQ_LEN // block_size, block_size, HEAD_DIM)

        def attend_block(query_block):
            scores = jnp.dot(query_block, jnp.transpose(key_head), preferred_element_type=jnp.float32) * score_scale
            scores = jnp.where(usable[None, :], scores, -jnp.inf)
            row_max = lax.optimization_barrier(jnp.max(scores, axis=1, keepdims=True))
            weights = jnp.exp(scores - row_max)
            numerator = jnp.dot(weights.astype(jnp.bfloat16), value_head, preferred_element_type=jnp.float32)
            return numerator / lax.optimization_barrier(jnp.sum(weights, axis=1, keepdims=True))
        return lax.map(attend_block, query_blocks).reshape(SEQ_LEN, HEAD_DIM)
    head_outputs = lax.map(attend_head, (split_heads(query_norm), split_heads(key_norm), split_heads(values)))
    attended = head_outputs.transpose(1, 0, 2).reshape(SEQ_LEN, FEATURES).astype(jnp.bfloat16)
    group_width = FEATURES // GROUPS
    attended_groups = attended.reshape(SEQ_LEN, GROUPS, group_width).transpose(1, 0, 2)
    weight_groups = out_weight.reshape(GROUPS, group_width, D)

    def add_group(running, pair):
        group_rows, group_weight = pair
        partial_sum = jnp.dot(group_rows, group_weight, preferred_element_type=jnp.float32).astype(jnp.bfloat16)
        partial_sum = lax.optimization_barrier(partial_sum)
        return (running + partial_sum.astype(jnp.float32), None)
    projected, _ = lax.scan(add_group, jnp.zeros((SEQ_LEN, D), jnp.float32), (attended_groups, weight_groups))
    return (gate[None, :] * projected).astype(jnp.bfloat16)
```

```python
import jax
import jax.numpy as jnp
from jax import lax
from jax.experimental import pallas as pl
from jax.experimental.pallas import tpu as pltpu
from jax.sharding import PartitionSpec as P

HEAD_DIM = 128


epsilon = 1e-06
lowest_score = -1e30


def normalize(matrix, squares, gain_row, feature_count):
    inverse_rms = lax.rsqrt(squares / feature_count + epsilon)
    return (matrix.astype(jnp.float32) * inverse_rms[:, None] * gain_row[None, :]).astype(
        jnp.bfloat16
    )


def absorb(carried, query_heads, key_block, value_block, offset, key_limit):
    running_sum, running_max, running_mass = carried
    scale_factor = query_heads.shape[2] ** (-0.5)
    scores = (
        jnp.einsum("qhd,khd->hqk", query_heads, key_block, preferred_element_type=jnp.float32)
        * scale_factor
    )
    position = offset + jnp.arange(key_block.shape[0], dtype=jnp.int32)
    usable = (position < key_limit)[None, None, :]
    masked = jnp.where(usable, scores, lowest_score)
    new_max = jnp.maximum(running_max, jnp.max(masked, axis=2))
    weights = jnp.where(usable, jnp.exp(masked - new_max[:, :, None]), 0.0)
    factor = jnp.exp(running_max - new_max)
    running_mass = running_mass * factor + jnp.sum(weights, axis=2)
    running_sum = running_sum * factor[:, :, None] + jnp.einsum(
        "hqk,khd->hqd",
        weights.astype(jnp.bfloat16),
        value_block,
        preferred_element_type=jnp.float32,
    )
    return (running_sum, new_max, running_mass)


def absorb_blocks(carried, query_heads, key_rows, value_rows, key_limit):
    row_total = key_rows.shape[0]
    block_size = 512
    block_count = row_total // block_size
    key_blocks = key_rows.reshape((block_count, block_size) + key_rows.shape[1:])
    value_blocks = value_rows.reshape((block_count, block_size) + value_rows.shape[1:])

    def absorb_block(running, triple):
        block_number, key_block, value_block = triple
        return (
            absorb(
                running, query_heads, key_block, value_block, block_number * block_size, key_limit
            ),
            None,
        )

    numbers = jnp.arange(block_count, dtype=jnp.int32)
    carried, _ = lax.scan(absorb_block, carried, (numbers, key_blocks, value_blocks))
    return carried


def visit(carried, query_heads, key_rows, value_rows, offset, key_limit):
    return lax.cond(
        offset < key_limit,
        lambda running: absorb_blocks(running, query_heads, key_rows, value_rows, key_limit),
        lambda running: running,
        carried,
    )


def local(queries, keys, values, out_weight, q_gain, k_gain, gate, valid_count):
    row_count = queries.shape[0]
    local_heads = queries.shape[1] // HEAD_DIM
    feature_count = queries.shape[1] * lax.axis_size(("head", "enc"))
    key_limit = valid_count[0]
    query_squares = jnp.sum(jnp.square(queries.astype(jnp.float32)), axis=1)
    key_squares = jnp.sum(jnp.square(keys.astype(jnp.float32)), axis=1)
    query_totals, key_totals = lax.psum((query_squares, key_squares), ("head", "enc"))
    query_heads = normalize(queries, query_totals, q_gain, feature_count).reshape(
        row_count, local_heads, HEAD_DIM
    )
    key_heads = normalize(keys, key_totals, k_gain, feature_count).reshape(
        row_count, local_heads, HEAD_DIM
    )
    value_heads = values.reshape(row_count, local_heads, HEAD_DIM)
    initial = (
        jnp.zeros((local_heads, row_count, HEAD_DIM), jnp.float32),
        jnp.full((local_heads, row_count), lowest_score, jnp.float32),
        jnp.zeros((local_heads, row_count), jnp.float32),
    )
    running_sum, running_max, running_mass = visit(
        initial,
        query_heads,
        lax.all_gather(key_heads, "seq", axis=0, tiled=True),
        lax.all_gather(value_heads, "seq", axis=0, tiled=True),
        jnp.int32(0),
        key_limit,
    )
    attended = (running_sum / running_mass[:, :, None]).transpose(1, 0, 2)
    attended = attended.reshape(row_count, local_heads * HEAD_DIM).astype(jnp.bfloat16)
    terms = jnp.dot(
        attended,
        lax.all_gather(out_weight, "seq", axis=1, tiled=True),
        preferred_element_type=jnp.float32,
    )
    summed = lax.psum_scatter(
        terms.astype(jnp.bfloat16), ("head", "enc"), scatter_dimension=1, tiled=True
    ).astype(jnp.float32)
    return (gate[None, :] * summed).astype(jnp.bfloat16)


def fused_kernel(
    limit_ref, q_ref, k_ref, v_ref, w_ref, qg_ref, kg_ref, gate_ref, out_ref,
    sums, k_out, q_out, k_all, v_all, q_all, w_line, w_all, att_out, att_all,
    sums_ss, sums_rs, a2a_ss, k_rs, v_rs, q_rs, fx_ss, fc_ss, fy_ss,
    wz_ss, wz_rs, wr_ss, ws_ss, ws_rs, wx_ss, az_ss, ay_ss, ac_ss, att_rs,
):
    enc_size = lax.axis_size("enc")
    groups = lax.axis_size("head") * enc_size
    rows = q_ref.shape[0]
    inner = lax.axis_size("seq") // groups
    outer = groups
    shares = outer // enc_size
    feature_count = q_ref.shape[1] * groups
    depth, width = w_ref.shape
    pieces = ws_rs.shape[2]
    piece_rows = depth // pieces
    s = lax.axis_index("seq")
    e = lax.axis_index("enc")
    h = lax.axis_index("head")
    g = h * enc_size + e
    a, b = s // inner, s % inner
    other_b, other_e, other_h = 1 - b, 1 - e, 1 - h
    catcher = a % enc_size
    is_catcher = e == catcher
    side = a // 2
    middle = (a + side) % 2
    pending = []

    def plane_of(which_side, is_middle):
        return which_side * (outer - 1) + is_middle * (1 - 2 * which_side)

    def send(src, dst, send_sem, recv_sem, seq_index, group):
        pltpu.make_async_remote_copy(
            src_ref=src, dst_ref=dst, send_sem=send_sem, recv_sem=recv_sem,
            device_id=(seq_index, group // enc_size, group % enc_size),
            device_id_type=pl.DeviceIdType.MESH,
        ).start()

    def wait(ref, sem):
        pltpu.make_async_copy(ref, ref, sem).wait()

    def push(src, dst, send_sem, recv_sem, seq_index, group, when=None):
        pending.append((when, src, send_sem))
        if when is None:
            send(src, dst, send_sem, recv_sem, seq_index, group)
        else:
            @pl.when(when)
            def _():
                send(src, dst, send_sem, recv_sem, seq_index, group)

    def push_or_keep(src, dst, send_sem, recv_sem, seq_index, group, here):
        @pl.when(here)
        def _():
            pltpu.make_async_copy(src, dst, recv_sem).start()

        push(src, dst, send_sem, recv_sem, seq_index, group, jnp.logical_not(here))

    def part_of(p):
        return pl.ds(p * piece_rows, piece_rows)

    def spread(block, origin, slot, p):
        src, dst = block.at[part_of(p)], w_all.at[b, g, part_of(p)]
        push(
            src, dst, ws_ss.at[slot, p, 0], ws_rs.at[b, g, p], a * inner + other_b, origin,
            None if p % 2 == 0 else origin // enc_size == h,
        )
        push_or_keep(
            src, dst, ws_ss.at[slot, p, 1], ws_rs.at[b, g, p], s, origin, origin == g
        )

    def spread_own(p):
        spread(w_ref, a, 0, p)

    def relay(k, p):
        for core in range(enc_size):
            group = other_h * enc_size + core
            piece = w_all.at[b, group, part_of(p)]
            here = g == (a if k is None else arrivals[k])

            @pl.when(here)
            def _():
                wait(piece, ws_rs.at[b, group, p])

            push(
                piece, piece, wx_ss.at[0 if k is None else k + 1, p, core], ws_rs.at[b, group, p],
                a * inner + other_b, g, here,
            )

    near = plane_of(side, 1 - middle)
    far_middle = plane_of(1 - side, 1)
    far_end = plane_of(1 - side, 0)
    own_end = plane_of(side, 0)

    def w_send(k, p):
        push(
            w_ref.at[part_of(p)], w_line.at[a, part_of(p)], wz_ss.at[k, p], wz_rs.at[a, p],
            (far_middle, near)[k] * inner + b, g,
        )

    arrivals = [
        jnp.where(middle == 1, far_middle, near),
        jnp.where(middle == 1, far_end, far_middle),
        jnp.where(middle == 1, near, far_end),
    ]

    def take(k, p):
        origin = arrivals[k]
        piece = w_line.at[origin, part_of(p)]
        wait(piece, wz_rs.at[origin, p])
        if k < 2:
            push(
                piece, piece, wr_ss.at[k, p], wz_rs.at[origin, p],
                own_end * inner + b, g, middle == 1,
            )
        spread(w_line.at[origin], origin, 1 + k, p)

    def share_of(turn):
        return (a // enc_size + turn) % shares

    def block_at(turn, core, column):
        return (share_of(turn) * enc_size + core) * inner + column

    stores = ((v_all, v_rs), (k_all, k_rs))

    def pass_on(kind, turn):
        store, store_rs = stores[kind]
        block = block_at(turn, e, b)
        wait(store.at[block], store_rs.at[block])
        push(
            store.at[block], store.at[block], fx_ss.at[kind, turn], store_rs.at[block],
            a * inner + other_b, g,
        )
        push(
            store.at[block], store.at[block], fc_ss.at[kind, turn], store_rs.at[block],
            s, h * enc_size + other_e,
        )

    def pass_across(kind, turn):
        store, store_rs = stores[kind]
        block = block_at(turn, e, other_b)
        wait(store.at[block], store_rs.at[block])
        push(
            store.at[block], store.at[block], fy_ss.at[kind, turn], store_rs.at[block],
            s, h * enc_size + other_e,
        )

    def gather_rest():
        for store, store_rs in stores:
            for turn in range(shares):
                for column in range(inner):
                    block = block_at(turn, other_e, column)
                    wait(store.at[block], store_rs.at[block])

    key_count = lax.axis_size("seq") * rows

    def attend(turn):
        share = share_of(turn + 1)
        plane = share * enc_size + e
        wait(q_all.at[share], q_rs.at[share])
        scores = lax.dot_general(
            q_all[share], k_all[...].reshape(key_count, HEAD_DIM), (((1,), (1,)), ((), ())),
            preferred_element_type=jnp.float32,
        ) * HEAD_DIM ** (-0.5)
        position = lax.broadcasted_iota(jnp.int32, scores.shape, 1)
        masked = jnp.where(position < limit_ref[0], scores, lowest_score)
        weights = jnp.exp(masked - jnp.max(masked, axis=1, keepdims=True))
        mass = jnp.sum(weights, axis=1, keepdims=True)
        mixed = jnp.dot(
            weights.astype(jnp.bfloat16), v_all[...].reshape(key_count, HEAD_DIM),
            preferred_element_type=jnp.float32,
        )
        att_out[turn] = (mixed / mass).astype(jnp.bfloat16)
        push_or_keep(
            att_out.at[turn], att_all.at[h, a], az_ss.at[turn], att_rs.at[h, a],
            plane * inner + b, g, plane == a,
        )

    def attended_on(ra):
        plane = (a + ra) % outer

        @pl.when(is_catcher)
        def _():
            wait(att_all.at[h, plane], att_rs.at[h, plane])

        push(
            att_all.at[h, plane], att_all.at[h, plane], ay_ss.at[ra], att_rs.at[h, plane],
            s, other_h * enc_size + e, is_catcher,
        )
        push(
            att_all.at[h, plane], att_all.at[h, plane], ac_ss.at[0, ra], att_rs.at[h, plane],
            s, h * enc_size + other_e, is_catcher,
        )

    def attended_across(ra):
        plane = (a + ra) % outer

        @pl.when(is_catcher)
        def _():
            wait(att_all.at[other_h, plane], att_rs.at[other_h, plane])

        push(
            att_all.at[other_h, plane], att_all.at[other_h, plane], ac_ss.at[1, ra],
            att_rs.at[other_h, plane], s, h * enc_size + other_e, is_catcher,
        )

    def attended_rest():
        @pl.when(jnp.logical_not(is_catcher))
        def _():
            for head in range(groups // enc_size):
                for plane in range(outer):
                    wait(att_all.at[head, plane], att_rs.at[head, plane])

    barrier = pltpu.get_barrier_semaphore()
    peers = []
    for rb in range(inner):
        for r in range(groups):
            if rb or r:
                peers.append((a * inner + (b + rb) % inner, (g + r) % groups))
    for ra in range(1, outer):
        for re in range(enc_size):
            peers.append((((a + ra) % outer) * inner + b, h * enc_size + re))
    for seq_index, group in peers:
        pl.semaphore_signal(
            barrier, inc=1, device_id=(seq_index, group // enc_size, group % enc_size),
            device_id_type=pl.DeviceIdType.MESH,
        )

    ones = jnp.ones((8, 2 * q_ref.shape[1]), jnp.bfloat16)

    def row_sums(ref):
        value = ref[...].astype(jnp.float32)
        square = value * value
        high = square.astype(jnp.bfloat16)
        low = (square - high.astype(jnp.float32)).astype(jnp.bfloat16)
        return lax.dot_general(
            ones, jnp.concatenate([high, low], axis=1), (((1,), (1,)), ((), ())),
            preferred_element_type=jnp.float32,
        )

    sums[g, 0:8, :] = row_sums(q_ref)
    sums[g, 8:16, :] = row_sums(k_ref)
    pl.semaphore_wait(barrier, len(peers))

    for r in range(1, groups):
        push(sums.at[g], sums.at[g], sums_ss.at[r], sums_rs.at[g], s, (g + r) % groups)

    def exchange(kind, i, src, dst, recv_sem):
        plane = e * 2 + i
        push_or_keep(
            src, dst, a2a_ss.at[kind, i], recv_sem, plane * inner + b, h * enc_size + catcher,
            jnp.logical_and(plane == a, is_catcher),
        )

    def send_values():
        for i in range(2):
            exchange(0, i, v_ref.at[:, pl.ds(i * HEAD_DIM, HEAD_DIM)], v_all.at[s], v_rs.at[s])

    def columns_of(rows_of_factors):
        parts, rest = [], rows_of_factors
        for _ in range(3):
            parts.append(rest.astype(jnp.bfloat16))
            rest = rest - parts[-1].astype(jnp.float32)
        row = lax.broadcasted_iota(jnp.int32, (48, 2 * HEAD_DIM), 0) % 16 // 8
        column = lax.broadcasted_iota(jnp.int32, (48, 2 * HEAD_DIM), 1) // HEAD_DIM
        pick = jnp.where(row == column, 0.125, 0.0).astype(jnp.bfloat16)
        return lax.dot_general(
            jnp.concatenate(parts, axis=0), pick, (((0,), (0,)), ((), ())),
            preferred_element_type=jnp.float32,
        )

    def normed(ref, factor, gain, i):
        columns = slice(i * HEAD_DIM, (i + 1) * HEAD_DIM)
        return (ref[:, columns].astype(jnp.float32) * factor * gain[:, columns]).astype(
            jnp.bfloat16
        )

    def send_normed():
        for r in range(1, groups):
            peer = (g + r) % groups
            wait(sums.at[peer], sums_rs.at[peer])
        total = sums[0]
        for r in range(1, groups):
            total = total + sums[r]
        factors = columns_of(lax.rsqrt(total / feature_count + epsilon))
        for i in range(2):
            k_out[i] = normed(k_ref, factors[:, HEAD_DIM:], kg_ref, i)
            exchange(1, i, k_out.at[i], k_all.at[s], k_rs.at[s])
        for i in range(2):
            q_out[i] = normed(q_ref, factors[:, :HEAD_DIM], qg_ref, i)
            exchange(2, i, q_out.at[i], q_all.at[a // enc_size], q_rs.at[a // enc_size])

    send_values()
    for p in range(0, 1):
        spread_own(p)
    for p in range(0, 1):
        w_send(0, p)
    for p in range(0, 1):
        w_send(1, p)
    for p in range(1, 2):
        w_send(1, p)
    for p in range(1, 2):
        spread_own(p)
    for p in range(1, 2):
        w_send(0, p)
    for p in range(2, 3):
        spread_own(p)
    send_normed()
    for turn in range(shares):
        pass_on(0, turn)
    for p in range(2, 3):
        w_send(0, p)
    for p in range(2, 3):
        w_send(1, p)
    for p in range(0, 1):
        take(0, p)
    for p in range(0, 1):
        take(1, p)
    for p in range(1, 2):
        take(0, p)
    for p in range(0, 1):
        take(2, p)
    for p in range(3, 4):
        spread_own(p)
    for turn in range(shares):
        pass_on(1, turn)
    for p in range(1, 2):
        take(1, p)
    for p in range(1, 2):
        take(2, p)
    for p in range(3, 4):
        w_send(0, p)
    for turn in range(shares):
        pass_across(0, turn)
    for p in range(2, 3):
        take(0, p)
    for p in range(2, 3):
        take(1, p)
    for turn in range(shares):
        pass_across(1, turn)
    relay(1, 1)
    gather_rest()
    for p in range(3, 4):
        w_send(1, p)
    relay(0, 1)
    for p in range(2, 3):
        take(2, p)
    relay(None, 1)
    attend(0)
    attend(1)
    relay(2, 1)
    for ra in range(outer):
        attended_on(ra)
    for p in range(3, 4):
        take(0, p)
    for p in range(3, 4):
        take(1, p)
    for p in range(3, 4):
        take(2, p)
    relay(0, 3)
    relay(None, 3)
    for ra in range(outer):
        attended_across(ra)
    relay(1, 3)
    attended_rest()
    relay(2, 3)

    for turn in range(inner):
        column = (b + turn) % inner
        summed = None
        for group in range(groups):
            for p in range(pieces):
                part = pl.ds(p * piece_rows, piece_rows)
                if p % 2 == 0:
                    wait(w_all.at[column, group, part], ws_rs.at[column, group, p])
                else:
                    @pl.when(jnp.logical_not(jnp.logical_and(column == b, group // enc_size != h)))
                    def _():
                        wait(w_all.at[column, group, part], ws_rs.at[column, group, p])
            head, first = group // enc_size, (group % enc_size) * 2
            lhs = jnp.concatenate([att_all[head, first], att_all[head, first + 1]], axis=1)
            term = jnp.dot(lhs, w_all[column, group], preferred_element_type=jnp.float32)
            term = term.astype(jnp.bfloat16).astype(jnp.float32)
            summed = term if summed is None else summed + term
        columns = pl.ds(pl.multiple_of(column * width, HEAD_DIM), width)
        out_ref[:, columns] = (gate_ref[:, columns] * summed).astype(jnp.bfloat16)

    for when, ref, sem in pending:
        if when is None:
            wait(ref, sem)
        else:
            @pl.when(when)
            def _():
                wait(ref, sem)


def fused(queries, keys, values, out_weight, q_gain, k_gain, gate, valid_count):
    seq_size = lax.axis_size("seq")
    enc_size = lax.axis_size("enc")
    heads = lax.axis_size("head")
    groups = heads * enc_size
    inner = seq_size // groups
    outer = groups
    rows = queries.shape[0]
    depth, width = out_weight.shape
    shares = outer // enc_size
    pieces = 4
    bf16, f32 = jnp.bfloat16, jnp.float32
    dma = pltpu.SemaphoreType.DMA
    vmem = pl.BlockSpec(memory_space=pltpu.VMEM)
    return pl.pallas_call(
        fused_kernel,
        out_shape=jax.ShapeDtypeStruct((rows, width * inner), bf16),
        in_specs=[pl.BlockSpec(memory_space=pltpu.SMEM)] + [vmem] * 7,
        out_specs=vmem,
        scratch_shapes=[
            pltpu.VMEM((groups, 16, rows), f32),
            pltpu.VMEM((2, rows, HEAD_DIM), bf16),
            pltpu.VMEM((2, rows, HEAD_DIM), bf16),
            pltpu.VMEM((seq_size, rows, HEAD_DIM), bf16),
            pltpu.VMEM((seq_size, rows, HEAD_DIM), bf16),
            pltpu.VMEM((shares, rows, HEAD_DIM), bf16),
            pltpu.VMEM((outer, depth, width), bf16),
            pltpu.VMEM((inner, groups, depth, width), bf16),
            pltpu.VMEM((shares, rows, HEAD_DIM), bf16),
            pltpu.VMEM((heads, outer, rows, HEAD_DIM), bf16),
            dma((groups,)), dma((groups,)),
            dma((3, 2)), dma((seq_size,)), dma((seq_size,)), dma((shares,)),
            dma((2, shares)), dma((2, shares)), dma((2, shares)),
            dma((2, pieces)), dma((outer, pieces)), dma((2, pieces)),
            dma((outer, pieces, 2)), dma((inner, groups, pieces)),
            dma((outer, pieces, enc_size)),
            dma((shares,)), dma((outer,)), dma((2, outer)), dma((heads, outer)),
        ],
        compiler_params=pltpu.CompilerParams(
            collective_id=0, has_side_effects=True, vmem_limit_bytes=56 * 2**20
        ),
    )(
        valid_count, queries, keys, values, out_weight,
        q_gain[None, :], k_gain[None, :], gate[None, :],
    )


def one_kernel_fits(mesh, queries, out_weight):
    sizes = mesh.shape
    seq_size, groups = sizes["seq"], sizes["head"] * sizes["enc"]
    return (
        sizes["enc"] == 2
        and sizes["head"] == 2
        and seq_size == 2 * groups
        and queries.shape[1] == 2 * groups * HEAD_DIM
        and (out_weight.shape[1] // seq_size) % HEAD_DIM == 0
    )


def solution(mesh):
    placed = (
        P("seq", ("head", "enc")),
        P("seq", ("head", "enc")),
        P("seq", ("head", "enc")),
        P(("head", "enc"), "seq"),
        P(("head", "enc")),
        P(("head", "enc")),
        P(("head", "enc")),
        P(),
    )

    def run(*arguments):
        body = fused if one_kernel_fits(mesh, arguments[0], arguments[3]) else local
        return jax.shard_map(
            body, mesh=mesh, in_specs=placed, out_specs=P("seq", ("head", "enc")),
            check_vma=False,
        )(*arguments)

    return run
```

```python
import jax
import jax.numpy as jnp
from jax import lax
from jax.experimental import pallas as pl
from jax.experimental.pallas import tpu as pltpu
from jax.sharding import PartitionSpec as P

HEAD_DIM = 128


epsilon = 1e-06
lowest_score = -1e30


def normalize(matrix, squares, gain_row, feature_count):
    inverse_rms = lax.rsqrt(squares / feature_count + epsilon)
    return (matrix.astype(jnp.float32) * inverse_rms[:, None] * gain_row[None, :]).astype(
        jnp.bfloat16
    )


def absorb(carried, query_heads, key_block, value_block, offset, key_limit):
    running_sum, running_max, running_mass = carried
    scale_factor = query_heads.shape[2] ** (-0.5)
    scores = (
        jnp.einsum("qhd,khd->hqk", query_heads, key_block, preferred_element_type=jnp.float32)
        * scale_factor
    )
    position = offset + jnp.arange(key_block.shape[0], dtype=jnp.int32)
    usable = (position < key_limit)[None, None, :]
    masked = jnp.where(usable, scores, lowest_score)
    new_max = jnp.maximum(running_max, jnp.max(masked, axis=2))
    weights = jnp.where(usable, jnp.exp(masked - new_max[:, :, None]), 0.0)
    factor = jnp.exp(running_max - new_max)
    running_mass = running_mass * factor + jnp.sum(weights, axis=2)
    running_sum = running_sum * factor[:, :, None] + jnp.einsum(
        "hqk,khd->hqd",
        weights.astype(jnp.bfloat16),
        value_block,
        preferred_element_type=jnp.float32,
    )
    return (running_sum, new_max, running_mass)


def absorb_blocks(carried, query_heads, key_rows, value_rows, key_limit):
    row_total = key_rows.shape[0]
    block_size = 512
    block_count = row_total // block_size
    key_blocks = key_rows.reshape((block_count, block_size) + key_rows.shape[1:])
    value_blocks = value_rows.reshape((block_count, block_size) + value_rows.shape[1:])

    def absorb_block(running, triple):
        block_number, key_block, value_block = triple
        return (
            absorb(
                running, query_heads, key_block, value_block, block_number * block_size, key_limit
            ),
            None,
        )

    numbers = jnp.arange(block_count, dtype=jnp.int32)
    carried, _ = lax.scan(absorb_block, carried, (numbers, key_blocks, value_blocks))
    return carried


def visit(carried, query_heads, key_rows, value_rows, offset, key_limit):
    return lax.cond(
        offset < key_limit,
        lambda running: absorb_blocks(running, query_heads, key_rows, value_rows, key_limit),
        lambda running: running,
        carried,
    )


def local(queries, keys, values, out_weight, q_gain, k_gain, gate, valid_count):
    row_count = queries.shape[0]
    local_heads = queries.shape[1] // HEAD_DIM
    feature_count = queries.shape[1] * lax.axis_size(("head", "enc"))
    key_limit = valid_count[0]
    query_squares = jnp.sum(jnp.square(queries.astype(jnp.float32)), axis=1)
    key_squares = jnp.sum(jnp.square(keys.astype(jnp.float32)), axis=1)
    query_totals, key_totals = lax.psum((query_squares, key_squares), ("head", "enc"))
    query_heads = normalize(queries, query_totals, q_gain, feature_count).reshape(
        row_count, local_heads, HEAD_DIM
    )
    key_heads = normalize(keys, key_totals, k_gain, feature_count).reshape(
        row_count, local_heads, HEAD_DIM
    )
    value_heads = values.reshape(row_count, local_heads, HEAD_DIM)
    initial = (
        jnp.zeros((local_heads, row_count, HEAD_DIM), jnp.float32),
        jnp.full((local_heads, row_count), lowest_score, jnp.float32),
        jnp.zeros((local_heads, row_count), jnp.float32),
    )
    running_sum, running_max, running_mass = visit(
        initial,
        query_heads,
        lax.all_gather(key_heads, "seq", axis=0, tiled=True),
        lax.all_gather(value_heads, "seq", axis=0, tiled=True),
        jnp.int32(0),
        key_limit,
    )
    attended = (running_sum / running_mass[:, :, None]).transpose(1, 0, 2)
    attended = attended.reshape(row_count, local_heads * HEAD_DIM).astype(jnp.bfloat16)
    terms = jnp.dot(
        attended,
        lax.all_gather(out_weight, "seq", axis=1, tiled=True),
        preferred_element_type=jnp.float32,
    )
    summed = lax.psum_scatter(
        terms.astype(jnp.bfloat16), ("head", "enc"), scatter_dimension=1, tiled=True
    ).astype(jnp.float32)
    return (gate[None, :] * summed).astype(jnp.bfloat16)


def fused_kernel(
    limit_hbm, q_hbm, k_hbm, v_hbm, w_hbm, qg_hbm, kg_hbm, gate_hbm, out_ref,
    limit_ref, q_ref, k_ref, v_ref, qg_ref, kg_ref, gate_ref, w_ref, in_sems,
    sums, k_out, q_out, k_all, v_all, q_all, w_line, w_all, att_out, att_all,
    sums_ss, sums_rs, a2a_ss, k_rs, v_rs, q_rs, fx_ss, fc_ss, fy_ss,
    wz_ss, wz_rs, wr_ss, ws_ss, ws_rs, wx_ss, az_ss, ay_ss, ac_ss, att_rs,
):
    enc_size = lax.axis_size("enc")
    groups = lax.axis_size("head") * enc_size
    rows = q_ref.shape[0]
    inner = lax.axis_size("seq") // groups
    outer = groups
    shares = outer // enc_size
    feature_count = q_ref.shape[1] * groups
    depth, width = w_ref.shape
    pieces = ws_rs.shape[2]
    piece_rows = depth // pieces
    s = lax.axis_index("seq")
    e = lax.axis_index("enc")
    h = lax.axis_index("head")
    g = h * enc_size + e
    a, b = s // inner, s % inner
    other_b, other_e, other_h = 1 - b, 1 - e, 1 - h
    catcher = a % enc_size
    is_catcher = e == catcher
    side = a // 2
    middle = (a + side) % 2
    pending = []

    def plane_of(which_side, is_middle):
        return which_side * (outer - 1) + is_middle * (1 - 2 * which_side)

    def send(src, dst, send_sem, recv_sem, seq_index, group):
        pltpu.make_async_remote_copy(
            src_ref=src, dst_ref=dst, send_sem=send_sem, recv_sem=recv_sem,
            device_id=(seq_index, group // enc_size, group % enc_size),
            device_id_type=pl.DeviceIdType.MESH,
        ).start()

    def wait(ref, sem):
        pltpu.make_async_copy(ref, ref, sem).wait()

    def push(src, dst, send_sem, recv_sem, seq_index, group, when=None):
        pending.append((when, src, send_sem))
        if when is None:
            send(src, dst, send_sem, recv_sem, seq_index, group)
        else:
            @pl.when(when)
            def _():
                send(src, dst, send_sem, recv_sem, seq_index, group)

    def push_or_keep(src, dst, send_sem, recv_sem, seq_index, group, here):
        @pl.when(here)
        def _():
            pltpu.make_async_copy(src, dst, recv_sem).start()

        push(src, dst, send_sem, recv_sem, seq_index, group, jnp.logical_not(here))

    def part_of(p):
        return pl.ds(p * piece_rows, piece_rows)

    def spread(block, origin, slot, p):
        src, dst = block.at[part_of(p)], w_all.at[b, g, part_of(p)]
        push(
            src, dst, ws_ss.at[slot, p, 0], ws_rs.at[b, g, p], a * inner + other_b, origin,
            None if p % 2 == 0 else origin // enc_size == h,
        )
        push_or_keep(
            src, dst, ws_ss.at[slot, p, 1], ws_rs.at[b, g, p], s, origin, origin == g
        )

    def spread_own(p):
        spread(w_ref, a, 0, p)

    def relay(k, p):
        for core in range(enc_size):
            group = other_h * enc_size + core
            piece = w_all.at[b, group, part_of(p)]
            here = g == (a if k is None else arrivals[k])

            @pl.when(here)
            def _():
                wait(piece, ws_rs.at[b, group, p])

            push(
                piece, piece, wx_ss.at[0 if k is None else k + 1, p, core], ws_rs.at[b, group, p],
                a * inner + other_b, g, here,
            )

    near = plane_of(side, 1 - middle)
    far_middle = plane_of(1 - side, 1)
    far_end = plane_of(1 - side, 0)
    own_end = plane_of(side, 0)

    def w_send(k, p):
        push(
            w_ref.at[part_of(p)], w_line.at[a, part_of(p)], wz_ss.at[k, p], wz_rs.at[a, p],
            (far_middle, near)[k] * inner + b, g,
        )

    arrivals = [
        jnp.where(middle == 1, far_middle, near),
        jnp.where(middle == 1, far_end, far_middle),
        jnp.where(middle == 1, near, far_end),
    ]

    def take(k, p):
        origin = arrivals[k]
        piece = w_line.at[origin, part_of(p)]
        wait(piece, wz_rs.at[origin, p])
        if k < 2:
            push(
                piece, piece, wr_ss.at[k, p], wz_rs.at[origin, p],
                own_end * inner + b, g, middle == 1,
            )
        spread(w_line.at[origin], origin, 1 + k, p)

    def share_of(turn):
        return (a // enc_size + turn) % shares

    def block_at(turn, core, column):
        return (share_of(turn) * enc_size + core) * inner + column

    stores = ((v_all, v_rs), (k_all, k_rs))

    def pass_on(kind, turn):
        store, store_rs = stores[kind]
        block = block_at(turn, e, b)
        wait(store.at[block], store_rs.at[block])
        push(
            store.at[block], store.at[block], fx_ss.at[kind, turn], store_rs.at[block],
            a * inner + other_b, g,
        )
        push(
            store.at[block], store.at[block], fc_ss.at[kind, turn], store_rs.at[block],
            s, h * enc_size + other_e,
        )

    def pass_across(kind, turn):
        store, store_rs = stores[kind]
        block = block_at(turn, e, other_b)
        wait(store.at[block], store_rs.at[block])
        push(
            store.at[block], store.at[block], fy_ss.at[kind, turn], store_rs.at[block],
            s, h * enc_size + other_e,
        )

    def gather_rest():
        for store, store_rs in stores:
            for turn in range(shares):
                for column in range(inner):
                    block = block_at(turn, other_e, column)
                    wait(store.at[block], store_rs.at[block])

    key_count = lax.axis_size("seq") * rows

    def attend(turn):
        share = share_of(turn + 1)
        plane = share * enc_size + e
        wait(q_all.at[share], q_rs.at[share])
        scores = lax.dot_general(
            q_all[share], k_all[...].reshape(key_count, HEAD_DIM), (((1,), (1,)), ((), ())),
            preferred_element_type=jnp.float32,
        ) * HEAD_DIM ** (-0.5)
        position = lax.broadcasted_iota(jnp.int32, scores.shape, 1)
        masked = jnp.where(position < limit_ref[0], scores, lowest_score)
        weights = jnp.exp(masked - jnp.max(masked, axis=1, keepdims=True))
        mass = jnp.sum(weights, axis=1, keepdims=True)
        mixed = jnp.dot(
            weights.astype(jnp.bfloat16), v_all[...].reshape(key_count, HEAD_DIM),
            preferred_element_type=jnp.float32,
        )
        att_out[turn] = (mixed / mass).astype(jnp.bfloat16)
        push_or_keep(
            att_out.at[turn], att_all.at[h, a], az_ss.at[turn], att_rs.at[h, a],
            plane * inner + b, g, plane == a,
        )

    def attended_on(ra):
        plane = (a + ra) % outer

        @pl.when(is_catcher)
        def _():
            wait(att_all.at[h, plane], att_rs.at[h, plane])

        push(
            att_all.at[h, plane], att_all.at[h, plane], ay_ss.at[ra], att_rs.at[h, plane],
            s, other_h * enc_size + e, is_catcher,
        )
        push(
            att_all.at[h, plane], att_all.at[h, plane], ac_ss.at[0, ra], att_rs.at[h, plane],
            s, h * enc_size + other_e, is_catcher,
        )

    def attended_across(ra):
        plane = (a + ra) % outer

        @pl.when(is_catcher)
        def _():
            wait(att_all.at[other_h, plane], att_rs.at[other_h, plane])

        push(
            att_all.at[other_h, plane], att_all.at[other_h, plane], ac_ss.at[1, ra],
            att_rs.at[other_h, plane], s, h * enc_size + other_e, is_catcher,
        )

    def attended_rest():
        @pl.when(jnp.logical_not(is_catcher))
        def _():
            for head in range(groups // enc_size):
                for plane in range(outer):
                    wait(att_all.at[head, plane], att_rs.at[head, plane])

    barrier = pltpu.get_barrier_semaphore()
    peers = []
    for rb in range(inner):
        for r in range(groups):
            if rb or r:
                peers.append((a * inner + (b + rb) % inner, (g + r) % groups))
    for ra in range(1, outer):
        for re in range(enc_size):
            peers.append((((a + ra) % outer) * inner + b, h * enc_size + re))
    for seq_index, group in peers:
        pl.semaphore_signal(
            barrier, inc=1, device_id=(seq_index, group // enc_size, group % enc_size),
            device_id_type=pl.DeviceIdType.MESH,
        )

    loads = [
        pltpu.make_async_copy(src, dst, in_sems.at[i])
        for i, (src, dst) in enumerate((
            (q_hbm, q_ref), (k_hbm, k_ref), (v_hbm, v_ref), (qg_hbm, qg_ref), (kg_hbm, kg_ref),
            (limit_hbm, limit_ref), (gate_hbm, gate_ref), (w_hbm, w_ref),
        ))
    ]
    for load in loads:
        load.start()

    ones = jnp.ones((8, 2 * q_ref.shape[1]), jnp.bfloat16)

    def row_sums(ref):
        value = ref[...].astype(jnp.float32)
        square = value * value
        high = square.astype(jnp.bfloat16)
        low = (square - high.astype(jnp.float32)).astype(jnp.bfloat16)
        return lax.dot_general(
            ones, jnp.concatenate([high, low], axis=1), (((1,), (1,)), ((), ())),
            preferred_element_type=jnp.float32,
        )

    loads[0].wait()
    sums[g, 0:8, :] = row_sums(q_ref)
    loads[1].wait()
    sums[g, 8:16, :] = row_sums(k_ref)
    for load in loads[2:]:
        load.wait()
    pl.semaphore_wait(barrier, len(peers))

    for r in range(1, groups):
        push(sums.at[g], sums.at[g], sums_ss.at[r], sums_rs.at[g], s, (g + r) % groups)

    def exchange(kind, i, src, dst, recv_sem):
        plane = e * 2 + i
        push_or_keep(
            src, dst, a2a_ss.at[kind, i], recv_sem, plane * inner + b, h * enc_size + catcher,
            jnp.logical_and(plane == a, is_catcher),
        )

    def send_values():
        for i in range(2):
            exchange(0, i, v_ref.at[:, pl.ds(i * HEAD_DIM, HEAD_DIM)], v_all.at[s], v_rs.at[s])

    def columns_of(rows_of_factors):
        parts, rest = [], rows_of_factors
        for _ in range(3):
            parts.append(rest.astype(jnp.bfloat16))
            rest = rest - parts[-1].astype(jnp.float32)
        row = lax.broadcasted_iota(jnp.int32, (48, 2 * HEAD_DIM), 0) % 16 // 8
        column = lax.broadcasted_iota(jnp.int32, (48, 2 * HEAD_DIM), 1) // HEAD_DIM
        pick = jnp.where(row == column, 0.125, 0.0).astype(jnp.bfloat16)
        return lax.dot_general(
            jnp.concatenate(parts, axis=0), pick, (((0,), (0,)), ((), ())),
            preferred_element_type=jnp.float32,
        )

    def normed(ref, factor, gain, i):
        columns = slice(i * HEAD_DIM, (i + 1) * HEAD_DIM)
        return (ref[:, columns].astype(jnp.float32) * factor * gain[:, columns]).astype(
            jnp.bfloat16
        )

    def send_normed():
        for r in range(1, groups):
            peer = (g + r) % groups
            wait(sums.at[peer], sums_rs.at[peer])
        total = sums[0]
        for r in range(1, groups):
            total = total + sums[r]
        factors = columns_of(lax.rsqrt(total / feature_count + epsilon))
        for i in range(2):
            k_out[i] = normed(k_ref, factors[:, HEAD_DIM:], kg_ref, i)
            exchange(1, i, k_out.at[i], k_all.at[s], k_rs.at[s])
        for i in range(2):
            q_out[i] = normed(q_ref, factors[:, :HEAD_DIM], qg_ref, i)

    def send_queries():
        for i in range(2):
            exchange(2, i, q_out.at[i], q_all.at[a // enc_size], q_rs.at[a // enc_size])

    send_values()
    for p in range(0, 1):
        w_send(1, p)
    for p in range(0, 1):
        w_send(0, p)
    for p in range(0, 1):
        spread_own(p)
    pass_on(0, 0)
    for p in range(1, 2):
        spread_own(p)
    send_normed()
    for p in range(0, 1):
        take(0, p)
    pass_on(1, 0)
    for p in range(1, 2):
        w_send(1, p)
    for p in range(2, 3):
        spread_own(p)
    for p in range(2, 3):
        w_send(1, p)
    for p in range(0, 1):
        take(1, p)
    for p in range(1, 2):
        w_send(0, p)
    pass_on(1, 1)
    for p in range(0, 1):
        take(2, p)
    pass_across(1, 0)
    for p in range(2, 3):
        w_send(0, p)
    pass_on(0, 1)
    for p in range(1, 2):
        take(0, p)
    send_queries()
    for p in range(1, 2):
        take(1, p)
    pass_across(1, 1)
    for p in range(2, 3):
        take(0, p)
    for p in range(1, 2):
        take(2, p)
    pass_across(0, 0)
    pass_across(0, 1)
    for p in range(3, 4):
        spread_own(p)
    relay(1, 1)
    for p in range(3, 4):
        w_send(0, p)
    for p in range(2, 3):
        take(1, p)
    for p in range(3, 4):
        w_send(1, p)
    for p in range(2, 3):
        take(2, p)
    gather_rest()
    relay(2, 1)
    attend(0)
    for p in range(3, 4):
        take(0, p)
    relay(None, 3)
    attend(1)
    relay(0, 1)
    relay(None, 1)
    attended_on(0)
    for p in range(3, 4):
        take(1, p)
    attended_on(1)
    relay(0, 3)
    for p in range(3, 4):
        take(2, p)
    attended_on(2)
    attended_on(3)
    attended_across(0)
    relay(1, 3)
    attended_across(1)
    attended_across(2)
    relay(2, 3)
    attended_across(3)
    attended_rest()

    for turn in range(inner):
        column = (b + turn) % inner
        summed = None
        for group in range(groups):
            for p in range(pieces):
                part = pl.ds(p * piece_rows, piece_rows)
                if p % 2 == 0:
                    wait(w_all.at[column, group, part], ws_rs.at[column, group, p])
                else:
                    @pl.when(jnp.logical_not(jnp.logical_and(column == b, group // enc_size != h)))
                    def _():
                        wait(w_all.at[column, group, part], ws_rs.at[column, group, p])
            head, first = group // enc_size, (group % enc_size) * 2
            lhs = jnp.concatenate([att_all[head, first], att_all[head, first + 1]], axis=1)
            term = jnp.dot(lhs, w_all[column, group], preferred_element_type=jnp.float32)
            term = term.astype(jnp.bfloat16).astype(jnp.float32)
            summed = term if summed is None else summed + term
        columns = pl.ds(pl.multiple_of(column * width, HEAD_DIM), width)
        out_ref[:, columns] = (gate_ref[:, columns] * summed).astype(jnp.bfloat16)

    for when, ref, sem in pending:
        if when is None:
            wait(ref, sem)
        else:
            @pl.when(when)
            def _():
                wait(ref, sem)


def fused(queries, keys, values, out_weight, q_gain, k_gain, gate, valid_count):
    seq_size = lax.axis_size("seq")
    enc_size = lax.axis_size("enc")
    heads = lax.axis_size("head")
    groups = heads * enc_size
    inner = seq_size // groups
    outer = groups
    rows = queries.shape[0]
    depth, width = out_weight.shape
    shares = outer // enc_size
    pieces = 4
    bf16, f32 = jnp.bfloat16, jnp.float32
    dma = pltpu.SemaphoreType.DMA
    hbm = pl.BlockSpec(memory_space=pl.ANY)
    return pl.pallas_call(
        fused_kernel,
        out_shape=pltpu.VMEM((rows, width * inner), bf16),
        in_specs=[hbm] * 8,
        out_specs=pl.BlockSpec(memory_space=pltpu.VMEM),
        scratch_shapes=[
            pltpu.SMEM((1,), jnp.int32),
            pltpu.VMEM(queries.shape, bf16),
            pltpu.VMEM(queries.shape, bf16),
            pltpu.VMEM(queries.shape, bf16),
            pltpu.VMEM((1, queries.shape[1]), f32),
            pltpu.VMEM((1, queries.shape[1]), f32),
            pltpu.VMEM((1, width * inner), f32),
            pltpu.VMEM((depth, width), bf16),
            dma((8,)),
            pltpu.VMEM((groups, 16, rows), f32),
            pltpu.VMEM((2, rows, HEAD_DIM), bf16),
            pltpu.VMEM((2, rows, HEAD_DIM), bf16),
            pltpu.VMEM((seq_size, rows, HEAD_DIM), bf16),
            pltpu.VMEM((seq_size, rows, HEAD_DIM), bf16),
            pltpu.VMEM((shares, rows, HEAD_DIM), bf16),
            pltpu.VMEM((outer, depth, width), bf16),
            pltpu.VMEM((inner, groups, depth, width), bf16),
            pltpu.VMEM((shares, rows, HEAD_DIM), bf16),
            pltpu.VMEM((heads, outer, rows, HEAD_DIM), bf16),
            dma((groups,)), dma((groups,)),
            dma((3, 2)), dma((seq_size,)), dma((seq_size,)), dma((shares,)),
            dma((2, shares)), dma((2, shares)), dma((2, shares)),
            dma((2, pieces)), dma((outer, pieces)), dma((2, pieces)),
            dma((outer, pieces, 2)), dma((inner, groups, pieces)),
            dma((outer, pieces, enc_size)),
            dma((shares,)), dma((outer,)), dma((2, outer)), dma((heads, outer)),
        ],
        compiler_params=pltpu.CompilerParams(
            collective_id=0, has_side_effects=True, vmem_limit_bytes=56 * 2**20
        ),
    )(
        valid_count, queries, keys, values, out_weight,
        q_gain[None, :], k_gain[None, :], gate[None, :],
    )


def one_kernel_fits(mesh, queries, out_weight):
    sizes = mesh.shape
    seq_size, groups = sizes["seq"], sizes["head"] * sizes["enc"]
    return (
        sizes["enc"] == 2
        and sizes["head"] == 2
        and seq_size == 2 * groups
        and queries.shape[1] == 2 * groups * HEAD_DIM
        and (out_weight.shape[1] // seq_size) % HEAD_DIM == 0
    )


def solution(mesh):
    placed = (
        P("seq", ("head", "enc")),
        P("seq", ("head", "enc")),
        P("seq", ("head", "enc")),
        P(("head", "enc"), "seq"),
        P(("head", "enc")),
        P(("head", "enc")),
        P(("head", "enc")),
        P(),
    )

    def run(*arguments):
        body = fused if one_kernel_fits(mesh, arguments[0], arguments[3]) else local
        return jax.shard_map(
            body, mesh=mesh, in_specs=placed, out_specs=P("seq", ("head", "enc")),
            check_vma=False,
        )(*arguments)

    return run
```

```python
import jax
import jax.numpy as jnp
from jax import lax
from jax.experimental import pallas as pl
from jax.experimental.pallas import tpu as pltpu
from jax.sharding import PartitionSpec as P

HEAD_DIM = 128


epsilon = 1e-06
lowest_score = -1e30


def normalize(matrix, squares, gain_row, feature_count):
    inverse_rms = lax.rsqrt(squares / feature_count + epsilon)
    return (matrix.astype(jnp.float32) * inverse_rms[:, None] * gain_row[None, :]).astype(
        jnp.bfloat16
    )


def absorb(carried, query_heads, key_block, value_block, offset, key_limit):
    running_sum, running_max, running_mass = carried
    scale_factor = query_heads.shape[2] ** (-0.5)
    scores = (
        jnp.einsum("qhd,khd->hqk", query_heads, key_block, preferred_element_type=jnp.float32)
        * scale_factor
    )
    position = offset + jnp.arange(key_block.shape[0], dtype=jnp.int32)
    usable = (position < key_limit)[None, None, :]
    masked = jnp.where(usable, scores, lowest_score)
    new_max = jnp.maximum(running_max, jnp.max(masked, axis=2))
    weights = jnp.where(usable, jnp.exp(masked - new_max[:, :, None]), 0.0)
    factor = jnp.exp(running_max - new_max)
    running_mass = running_mass * factor + jnp.sum(weights, axis=2)
    running_sum = running_sum * factor[:, :, None] + jnp.einsum(
        "hqk,khd->hqd",
        weights.astype(jnp.bfloat16),
        value_block,
        preferred_element_type=jnp.float32,
    )
    return (running_sum, new_max, running_mass)


def absorb_blocks(carried, query_heads, key_rows, value_rows, key_limit):
    row_total = key_rows.shape[0]
    block_size = 512
    block_count = row_total // block_size
    key_blocks = key_rows.reshape((block_count, block_size) + key_rows.shape[1:])
    value_blocks = value_rows.reshape((block_count, block_size) + value_rows.shape[1:])

    def absorb_block(running, triple):
        block_number, key_block, value_block = triple
        return (
            absorb(
                running, query_heads, key_block, value_block, block_number * block_size, key_limit
            ),
            None,
        )

    numbers = jnp.arange(block_count, dtype=jnp.int32)
    carried, _ = lax.scan(absorb_block, carried, (numbers, key_blocks, value_blocks))
    return carried


def visit(carried, query_heads, key_rows, value_rows, offset, key_limit):
    return lax.cond(
        offset < key_limit,
        lambda running: absorb_blocks(running, query_heads, key_rows, value_rows, key_limit),
        lambda running: running,
        carried,
    )


def local(queries, keys, values, out_weight, q_gain, k_gain, gate, valid_count):
    row_count = queries.shape[0]
    local_heads = queries.shape[1] // HEAD_DIM
    feature_count = queries.shape[1] * lax.axis_size(("head", "enc"))
    key_limit = valid_count[0]
    query_squares = jnp.sum(jnp.square(queries.astype(jnp.float32)), axis=1)
    key_squares = jnp.sum(jnp.square(keys.astype(jnp.float32)), axis=1)
    query_totals, key_totals = lax.psum((query_squares, key_squares), ("head", "enc"))
    query_heads = normalize(queries, query_totals, q_gain, feature_count).reshape(
        row_count, local_heads, HEAD_DIM
    )
    key_heads = normalize(keys, key_totals, k_gain, feature_count).reshape(
        row_count, local_heads, HEAD_DIM
    )
    value_heads = values.reshape(row_count, local_heads, HEAD_DIM)
    initial = (
        jnp.zeros((local_heads, row_count, HEAD_DIM), jnp.float32),
        jnp.full((local_heads, row_count), lowest_score, jnp.float32),
        jnp.zeros((local_heads, row_count), jnp.float32),
    )
    running_sum, running_max, running_mass = visit(
        initial,
        query_heads,
        lax.all_gather(key_heads, "seq", axis=0, tiled=True),
        lax.all_gather(value_heads, "seq", axis=0, tiled=True),
        jnp.int32(0),
        key_limit,
    )
    attended = (running_sum / running_mass[:, :, None]).transpose(1, 0, 2)
    attended = attended.reshape(row_count, local_heads * HEAD_DIM).astype(jnp.bfloat16)
    terms = jnp.dot(
        attended,
        lax.all_gather(out_weight, "seq", axis=1, tiled=True),
        preferred_element_type=jnp.float32,
    )
    summed = lax.psum_scatter(
        terms.astype(jnp.bfloat16), ("head", "enc"), scatter_dimension=1, tiled=True
    ).astype(jnp.float32)
    return (gate[None, :] * summed).astype(jnp.bfloat16)


def fused_kernel(
    limit_hbm, q_hbm, k_hbm, v_hbm, w_hbm, qg_hbm, kg_hbm, gate_hbm, out_ref,
    limit_ref, q_ref, k_ref, v_ref, qg_ref, kg_ref, gate_ref, w_ref, in_sems,
    sums, k_out, q_out, k_all, v_all, q_all, w_line, w_all, att_out, att_all,
    sums_ss, sums_rs, a2a_ss, k_rs, v_rs, q_rs, fx_ss, fc_ss, fy_ss,
    wz_ss, wz_rs, wr_ss, ws_ss, ws_rs, wx_ss, az_ss, ay_ss, ac_ss, att_rs,
):
    enc_size = lax.axis_size("enc")
    groups = lax.axis_size("head") * enc_size
    rows = q_ref.shape[0]
    inner = lax.axis_size("seq") // groups
    outer = groups
    shares = outer // enc_size
    feature_count = q_ref.shape[1] * groups
    depth, width = w_ref.shape
    pieces = ws_rs.shape[2]
    piece_rows = depth // pieces
    s = lax.axis_index("seq")
    e = lax.axis_index("enc")
    h = lax.axis_index("head")
    g = h * enc_size + e
    a, b = s // inner, s % inner
    other_b, other_e, other_h = 1 - b, 1 - e, 1 - h
    catcher = a % enc_size
    is_catcher = e == catcher
    side = a // 2
    middle = (a + side) % 2
    pending = []

    def plane_of(which_side, is_middle):
        return which_side * (outer - 1) + is_middle * (1 - 2 * which_side)

    def send(src, dst, send_sem, recv_sem, seq_index, group):
        pltpu.make_async_remote_copy(
            src_ref=src, dst_ref=dst, send_sem=send_sem, recv_sem=recv_sem,
            device_id=(seq_index, group // enc_size, group % enc_size),
            device_id_type=pl.DeviceIdType.MESH,
        ).start()

    def wait(ref, sem):
        pltpu.make_async_copy(ref, ref, sem).wait()

    def push(src, dst, send_sem, recv_sem, seq_index, group, when=None):
        pending.append((when, src, send_sem))
        if when is None:
            send(src, dst, send_sem, recv_sem, seq_index, group)
        else:
            @pl.when(when)
            def _():
                send(src, dst, send_sem, recv_sem, seq_index, group)

    def push_or_keep(src, dst, send_sem, recv_sem, seq_index, group, here):
        @pl.when(here)
        def _():
            pltpu.make_async_copy(src, dst, recv_sem).start()

        push(src, dst, send_sem, recv_sem, seq_index, group, jnp.logical_not(here))

    def part_of(p):
        return pl.ds(p * piece_rows, piece_rows)

    def spread(block, origin, slot, p):
        src, dst = block.at[part_of(p)], w_all.at[b, g, part_of(p)]
        push(
            src, dst, ws_ss.at[slot, p, 0], ws_rs.at[b, g, p], a * inner + other_b, origin,
            None if p % 2 == 0 else origin // enc_size == h,
        )
        push_or_keep(
            src, dst, ws_ss.at[slot, p, 1], ws_rs.at[b, g, p], s, origin, origin == g
        )

    def spread_own(p):
        spread(w_ref, a, 0, p)

    def relay(k, p):
        for core in range(enc_size):
            group = other_h * enc_size + core
            piece = w_all.at[b, group, part_of(p)]
            here = g == (a if k is None else arrivals[k])

            @pl.when(here)
            def _():
                wait(piece, ws_rs.at[b, group, p])

            push(
                piece, piece, wx_ss.at[0 if k is None else k + 1, p, core], ws_rs.at[b, group, p],
                a * inner + other_b, g, here,
            )

    near = plane_of(side, 1 - middle)
    far_middle = plane_of(1 - side, 1)
    far_end = plane_of(1 - side, 0)
    own_end = plane_of(side, 0)

    def w_send(k, p):
        push(
            w_ref.at[part_of(p)], w_line.at[a, part_of(p)], wz_ss.at[k, p], wz_rs.at[a, p],
            (far_middle, near)[k] * inner + b, g,
        )

    arrivals = [
        jnp.where(middle == 1, far_middle, near),
        jnp.where(middle == 1, far_end, far_middle),
        jnp.where(middle == 1, near, far_end),
    ]

    def take(k, p):
        origin = arrivals[k]
        piece = w_line.at[origin, part_of(p)]
        wait(piece, wz_rs.at[origin, p])
        if k < 2:
            push(
                piece, piece, wr_ss.at[k, p], wz_rs.at[origin, p],
                own_end * inner + b, g, middle == 1,
            )
        spread(w_line.at[origin], origin, 1 + k, p)

    def share_of(turn):
        return (a // enc_size + turn) % shares

    def block_at(turn, core, column):
        return (share_of(turn) * enc_size + core) * inner + column

    stores = ((v_all, v_rs), (k_all, k_rs))

    def pass_on(kind, turn):
        store, store_rs = stores[kind]
        block = block_at(turn, e, b)
        wait(store.at[block], store_rs.at[block])
        push(
            store.at[block], store.at[block], fx_ss.at[kind, turn], store_rs.at[block],
            a * inner + other_b, g,
        )
        push(
            store.at[block], store.at[block], fc_ss.at[kind, turn], store_rs.at[block],
            s, h * enc_size + other_e,
        )

    def pass_across(kind, turn):
        store, store_rs = stores[kind]
        block = block_at(turn, e, other_b)
        wait(store.at[block], store_rs.at[block])
        push(
            store.at[block], store.at[block], fy_ss.at[kind, turn], store_rs.at[block],
            s, h * enc_size + other_e,
        )

    def gather_rest():
        for store, store_rs in stores:
            for turn in range(shares):
                for column in range(inner):
                    block = block_at(turn, other_e, column)
                    wait(store.at[block], store_rs.at[block])

    key_count = lax.axis_size("seq") * rows

    def attend(turn):
        share = share_of(turn + 1)
        plane = share * enc_size + e
        wait(q_all.at[share], q_rs.at[share])
        scores = lax.dot_general(
            q_all[share], k_all[...].reshape(key_count, HEAD_DIM), (((1,), (1,)), ((), ())),
            preferred_element_type=jnp.float32,
        ) * HEAD_DIM ** (-0.5)
        position = lax.broadcasted_iota(jnp.int32, scores.shape, 1)
        masked = jnp.where(position < limit_ref[0], scores, lowest_score)
        weights = jnp.exp(masked - jnp.max(masked, axis=1, keepdims=True))
        mass = jnp.sum(weights, axis=1, keepdims=True)
        mixed = jnp.dot(
            weights.astype(jnp.bfloat16), v_all[...].reshape(key_count, HEAD_DIM),
            preferred_element_type=jnp.float32,
        )
        att_out[turn] = (mixed / mass).astype(jnp.bfloat16)
        push_or_keep(
            att_out.at[turn], att_all.at[h, a], az_ss.at[turn], att_rs.at[h, a],
            plane * inner + b, g, plane == a,
        )

    def attended_on(ra):
        plane = (a + ra) % outer

        @pl.when(is_catcher)
        def _():
            wait(att_all.at[h, plane], att_rs.at[h, plane])

        push(
            att_all.at[h, plane], att_all.at[h, plane], ay_ss.at[ra], att_rs.at[h, plane],
            s, other_h * enc_size + e, is_catcher,
        )
        push(
            att_all.at[h, plane], att_all.at[h, plane], ac_ss.at[0, ra], att_rs.at[h, plane],
            s, h * enc_size + other_e, is_catcher,
        )

    def attended_across(ra):
        plane = (a + ra) % outer

        @pl.when(is_catcher)
        def _():
            wait(att_all.at[other_h, plane], att_rs.at[other_h, plane])

        push(
            att_all.at[other_h, plane], att_all.at[other_h, plane], ac_ss.at[1, ra],
            att_rs.at[other_h, plane], s, h * enc_size + other_e, is_catcher,
        )

    def attended_rest():
        @pl.when(jnp.logical_not(is_catcher))
        def _():
            for head in range(groups // enc_size):
                for plane in range(outer):
                    wait(att_all.at[head, plane], att_rs.at[head, plane])

    barrier = pltpu.get_barrier_semaphore()
    peers = []
    for rb in range(inner):
        for r in range(groups):
            if rb or r:
                peers.append((a * inner + (b + rb) % inner, (g + r) % groups))
    for ra in range(1, outer):
        for re in range(enc_size):
            peers.append((((a + ra) % outer) * inner + b, h * enc_size + re))
    for seq_index, group in peers:
        pl.semaphore_signal(
            barrier, inc=1, device_id=(seq_index, group // enc_size, group % enc_size),
            device_id_type=pl.DeviceIdType.MESH,
        )

    loads = [
        pltpu.make_async_copy(src, dst, in_sems.at[i])
        for i, (src, dst) in enumerate((
            (q_hbm, q_ref), (k_hbm, k_ref), (v_hbm, v_ref), (qg_hbm, qg_ref), (kg_hbm, kg_ref),
            (limit_hbm, limit_ref), (gate_hbm, gate_ref), (w_hbm, w_ref),
        ))
    ]
    for load in loads:
        load.start()

    ones = jnp.ones((8, 2 * q_ref.shape[1]), jnp.bfloat16)

    def row_sums(ref):
        value = ref[...].astype(jnp.float32)
        square = value * value
        high = square.astype(jnp.bfloat16)
        low = (square - high.astype(jnp.float32)).astype(jnp.bfloat16)
        return lax.dot_general(
            ones, jnp.concatenate([high, low], axis=1), (((1,), (1,)), ((), ())),
            preferred_element_type=jnp.float32,
        )

    loads[0].wait()
    sums[g, 0:8, :] = row_sums(q_ref)
    loads[1].wait()
    sums[g, 8:16, :] = row_sums(k_ref)
    for load in loads[2:]:
        load.wait()
    pl.semaphore_wait(barrier, len(peers))

    for r in range(1, groups):
        push(sums.at[g], sums.at[g], sums_ss.at[r], sums_rs.at[g], s, (g + r) % groups)

    def exchange(kind, i, src, dst, recv_sem):
        plane = e * 2 + i
        push_or_keep(
            src, dst, a2a_ss.at[kind, i], recv_sem, plane * inner + b, h * enc_size + catcher,
            jnp.logical_and(plane == a, is_catcher),
        )

    def send_values():
        for i in range(2):
            exchange(0, i, v_ref.at[:, pl.ds(i * HEAD_DIM, HEAD_DIM)], v_all.at[s], v_rs.at[s])

    def columns_of(rows_of_factors):
        parts, rest = [], rows_of_factors
        for _ in range(3):
            parts.append(rest.astype(jnp.bfloat16))
            rest = rest - parts[-1].astype(jnp.float32)
        row = lax.broadcasted_iota(jnp.int32, (48, 2 * HEAD_DIM), 0) % 16 // 8
        column = lax.broadcasted_iota(jnp.int32, (48, 2 * HEAD_DIM), 1) // HEAD_DIM
        pick = jnp.where(row == column, 0.125, 0.0).astype(jnp.bfloat16)
        return lax.dot_general(
            jnp.concatenate(parts, axis=0), pick, (((0,), (0,)), ((), ())),
            preferred_element_type=jnp.float32,
        )

    def normed(ref, factor, gain, i):
        columns = slice(i * HEAD_DIM, (i + 1) * HEAD_DIM)
        return (ref[:, columns].astype(jnp.float32) * factor * gain[:, columns]).astype(
            jnp.bfloat16
        )

    def send_normed():
        for r in range(1, groups):
            peer = (g + r) % groups
            wait(sums.at[peer], sums_rs.at[peer])
        total = sums[0]
        for r in range(1, groups):
            total = total + sums[r]
        factors = columns_of(lax.rsqrt(total / feature_count + epsilon))
        for i in range(2):
            k_out[i] = normed(k_ref, factors[:, HEAD_DIM:], kg_ref, i)
            exchange(1, i, k_out.at[i], k_all.at[s], k_rs.at[s])
        for i in range(2):
            q_out[i] = normed(q_ref, factors[:, :HEAD_DIM], qg_ref, i)

    def send_queries():
        for i in range(2):
            exchange(2, i, q_out.at[i], q_all.at[a // enc_size], q_rs.at[a // enc_size])

    send_values()
    for p in range(0, 1):
        w_send(1, p)
    for p in range(0, 1):
        w_send(0, p)
    for p in range(0, 1):
        spread_own(p)
    pass_on(0, 0)
    for p in range(1, 2):
        spread_own(p)
    send_normed()
    for p in range(0, 1):
        take(0, p)
    pass_on(1, 0)
    for p in range(1, 2):
        w_send(1, p)
    for p in range(2, 3):
        spread_own(p)
    for p in range(2, 3):
        w_send(1, p)
    for p in range(0, 1):
        take(1, p)
    for p in range(1, 2):
        w_send(0, p)
    pass_on(1, 1)
    for p in range(0, 1):
        take(2, p)
    pass_across(1, 0)
    for p in range(2, 3):
        w_send(0, p)
    pass_on(0, 1)
    for p in range(1, 2):
        take(0, p)
    send_queries()
    for p in range(1, 2):
        take(1, p)
    pass_across(1, 1)
    for p in range(2, 3):
        take(0, p)
    for p in range(1, 2):
        take(2, p)
    pass_across(0, 0)
    pass_across(0, 1)
    for p in range(3, 4):
        spread_own(p)
    relay(1, 1)
    for p in range(3, 4):
        w_send(0, p)
    for p in range(2, 3):
        take(1, p)
    for p in range(3, 4):
        w_send(1, p)
    for p in range(2, 3):
        take(2, p)
    gather_rest()
    relay(2, 1)
    attend(0)
    for p in range(3, 4):
        take(0, p)
    relay(None, 3)
    attend(1)
    relay(0, 1)
    relay(None, 1)
    attended_on(0)
    for p in range(3, 4):
        take(1, p)
    attended_on(1)
    relay(0, 3)
    for p in range(3, 4):
        take(2, p)
    attended_on(2)
    attended_on(3)
    attended_across(0)
    relay(1, 3)
    attended_across(1)
    attended_across(2)
    relay(2, 3)
    attended_across(3)
    attended_rest()

    for turn in range(inner):
        column = (b + turn) % inner
        summed = None
        for group in range(groups):
            for p in range(pieces):
                part = pl.ds(p * piece_rows, piece_rows)
                if p % 2 == 0:
                    wait(w_all.at[column, group, part], ws_rs.at[column, group, p])
                else:
                    @pl.when(jnp.logical_not(jnp.logical_and(column == b, group // enc_size != h)))
                    def _():
                        wait(w_all.at[column, group, part], ws_rs.at[column, group, p])
            head, first = group // enc_size, (group % enc_size) * 2
            lhs = jnp.concatenate([att_all[head, first], att_all[head, first + 1]], axis=1)
            term = jnp.dot(lhs, w_all[column, group], preferred_element_type=jnp.float32)
            term = term.astype(jnp.bfloat16).astype(jnp.float32)
            summed = term if summed is None else summed + term
        columns = pl.ds(pl.multiple_of(column * width, HEAD_DIM), width)
        gates = jnp.where(column == 0, gate_ref[:width][None, :], gate_ref[width:][None, :])
        out_ref[:, columns] = (gates * summed).astype(jnp.bfloat16)

    for when, ref, sem in pending:
        if when is None:
            wait(ref, sem)
        else:
            @pl.when(when)
            def _():
                wait(ref, sem)


def fused(queries, keys, values, out_weight, q_gain, k_gain, gate, valid_count):
    seq_size = lax.axis_size("seq")
    enc_size = lax.axis_size("enc")
    heads = lax.axis_size("head")
    groups = heads * enc_size
    inner = seq_size // groups
    outer = groups
    rows = queries.shape[0]
    depth, width = out_weight.shape
    shares = outer // enc_size
    pieces = 4
    bf16, f32 = jnp.bfloat16, jnp.float32
    dma = pltpu.SemaphoreType.DMA
    hbm = pl.BlockSpec(memory_space=pl.ANY)
    return pl.pallas_call(
        fused_kernel,
        out_shape=pltpu.VMEM((rows, width * inner), bf16),
        in_specs=[hbm] * 8,
        out_specs=pl.BlockSpec(memory_space=pltpu.VMEM),
        scratch_shapes=[
            pltpu.SMEM((1,), jnp.int32),
            pltpu.VMEM(queries.shape, bf16),
            pltpu.VMEM(queries.shape, bf16),
            pltpu.VMEM(queries.shape, bf16),
            pltpu.VMEM((1, queries.shape[1]), f32),
            pltpu.VMEM((1, queries.shape[1]), f32),
            pltpu.VMEM((width * inner,), f32),
            pltpu.VMEM((depth, width), bf16),
            dma((8,)),
            pltpu.VMEM((groups, 16, rows), f32),
            pltpu.VMEM((2, rows, HEAD_DIM), bf16),
            pltpu.VMEM((2, rows, HEAD_DIM), bf16),
            pltpu.VMEM((seq_size, rows, HEAD_DIM), bf16),
            pltpu.VMEM((seq_size, rows, HEAD_DIM), bf16),
            pltpu.VMEM((shares, rows, HEAD_DIM), bf16),
            pltpu.VMEM((outer, depth, width), bf16),
            pltpu.VMEM((inner, groups, depth, width), bf16),
            pltpu.VMEM((shares, rows, HEAD_DIM), bf16),
            pltpu.VMEM((heads, outer, rows, HEAD_DIM), bf16),
            dma((groups,)), dma((groups,)),
            dma((3, 2)), dma((seq_size,)), dma((seq_size,)), dma((shares,)),
            dma((2, shares)), dma((2, shares)), dma((2, shares)),
            dma((2, pieces)), dma((outer, pieces)), dma((2, pieces)),
            dma((outer, pieces, 2)), dma((inner, groups, pieces)),
            dma((outer, pieces, enc_size)),
            dma((shares,)), dma((outer,)), dma((2, outer)), dma((heads, outer)),
        ],
        compiler_params=pltpu.CompilerParams(
            collective_id=0, has_side_effects=True, vmem_limit_bytes=56 * 2**20
        ),
    )(
        valid_count, queries, keys, values, out_weight,
        q_gain[None, :], k_gain[None, :], gate,
    )


def one_kernel_fits(mesh, queries, out_weight):
    sizes = mesh.shape
    seq_size, groups = sizes["seq"], sizes["head"] * sizes["enc"]
    return (
        sizes["enc"] == 2
        and sizes["head"] == 2
        and seq_size == 2 * groups
        and queries.shape[1] == 2 * groups * HEAD_DIM
        and (out_weight.shape[1] // seq_size) % HEAD_DIM == 0
    )


def solution(mesh):
    placed = (
        P("seq", ("head", "enc")),
        P("seq", ("head", "enc")),
        P("seq", ("head", "enc")),
        P(("head", "enc"), "seq"),
        P(("head", "enc")),
        P(("head", "enc")),
        P(("head", "enc")),
        P(),
    )

    def run(*arguments):
        body = fused if one_kernel_fits(mesh, arguments[0], arguments[3]) else local
        return jax.shard_map(
            body, mesh=mesh, in_specs=placed, out_specs=P("seq", ("head", "enc")),
            check_vma=False,
        )(*arguments)

    return run
```

```python
import jax
import jax.numpy as jnp
from jax import lax
from jax.experimental import pallas as pl
from jax.experimental.pallas import tpu as pltpu
from jax.sharding import PartitionSpec as P

HEAD_DIM = 128


epsilon = 1e-06
lowest_score = -1e30


def normalize(matrix, squares, gain_row, feature_count):
    inverse_rms = lax.rsqrt(squares / feature_count + epsilon)
    return (matrix.astype(jnp.float32) * inverse_rms[:, None] * gain_row[None, :]).astype(
        jnp.bfloat16
    )


def absorb(carried, query_heads, key_block, value_block, offset, key_limit):
    running_sum, running_max, running_mass = carried
    scale_factor = query_heads.shape[2] ** (-0.5)
    scores = (
        jnp.einsum("qhd,khd->hqk", query_heads, key_block, preferred_element_type=jnp.float32)
        * scale_factor
    )
    position = offset + jnp.arange(key_block.shape[0], dtype=jnp.int32)
    usable = (position < key_limit)[None, None, :]
    masked = jnp.where(usable, scores, lowest_score)
    new_max = jnp.maximum(running_max, jnp.max(masked, axis=2))
    weights = jnp.where(usable, jnp.exp(masked - new_max[:, :, None]), 0.0)
    factor = jnp.exp(running_max - new_max)
    running_mass = running_mass * factor + jnp.sum(weights, axis=2)
    running_sum = running_sum * factor[:, :, None] + jnp.einsum(
        "hqk,khd->hqd",
        weights.astype(jnp.bfloat16),
        value_block,
        preferred_element_type=jnp.float32,
    )
    return (running_sum, new_max, running_mass)


def absorb_blocks(carried, query_heads, key_rows, value_rows, key_limit):
    row_total = key_rows.shape[0]
    block_size = 512
    block_count = row_total // block_size
    key_blocks = key_rows.reshape((block_count, block_size) + key_rows.shape[1:])
    value_blocks = value_rows.reshape((block_count, block_size) + value_rows.shape[1:])

    def absorb_block(running, triple):
        block_number, key_block, value_block = triple
        return (
            absorb(
                running, query_heads, key_block, value_block, block_number * block_size, key_limit
            ),
            None,
        )

    numbers = jnp.arange(block_count, dtype=jnp.int32)
    carried, _ = lax.scan(absorb_block, carried, (numbers, key_blocks, value_blocks))
    return carried


def visit(carried, query_heads, key_rows, value_rows, offset, key_limit):
    return lax.cond(
        offset < key_limit,
        lambda running: absorb_blocks(running, query_heads, key_rows, value_rows, key_limit),
        lambda running: running,
        carried,
    )


def local(queries, keys, values, out_weight, q_gain, k_gain, gate, valid_count):
    row_count = queries.shape[0]
    local_heads = queries.shape[1] // HEAD_DIM
    feature_count = queries.shape[1] * lax.axis_size(("head", "enc"))
    key_limit = valid_count[0]
    query_squares = jnp.sum(jnp.square(queries.astype(jnp.float32)), axis=1)
    key_squares = jnp.sum(jnp.square(keys.astype(jnp.float32)), axis=1)
    query_totals, key_totals = lax.psum((query_squares, key_squares), ("head", "enc"))
    query_heads = normalize(queries, query_totals, q_gain, feature_count).reshape(
        row_count, local_heads, HEAD_DIM
    )
    key_heads = normalize(keys, key_totals, k_gain, feature_count).reshape(
        row_count, local_heads, HEAD_DIM
    )
    value_heads = values.reshape(row_count, local_heads, HEAD_DIM)
    initial = (
        jnp.zeros((local_heads, row_count, HEAD_DIM), jnp.float32),
        jnp.full((local_heads, row_count), lowest_score, jnp.float32),
        jnp.zeros((local_heads, row_count), jnp.float32),
    )
    running_sum, running_max, running_mass = visit(
        initial,
        query_heads,
        lax.all_gather(key_heads, "seq", axis=0, tiled=True),
        lax.all_gather(value_heads, "seq", axis=0, tiled=True),
        jnp.int32(0),
        key_limit,
    )
    attended = (running_sum / running_mass[:, :, None]).transpose(1, 0, 2)
    attended = attended.reshape(row_count, local_heads * HEAD_DIM).astype(jnp.bfloat16)
    terms = jnp.dot(
        attended,
        lax.all_gather(out_weight, "seq", axis=1, tiled=True),
        preferred_element_type=jnp.float32,
    )
    summed = lax.psum_scatter(
        terms.astype(jnp.bfloat16), ("head", "enc"), scatter_dimension=1, tiled=True
    ).astype(jnp.float32)
    return (gate[None, :] * summed).astype(jnp.bfloat16)


def fused_kernel(
    limit_hbm, q_hbm, k_hbm, v_hbm, w_hbm, qg_hbm, kg_hbm, gate_hbm, out_ref,
    limit_ref, q_ref, k_ref, v_ref, qg_ref, kg_ref, gate_ref, w_ref, in_sems,
    sums, k_out, q_out, k_all, v_all, q_all, w_line, w_all, att_out, att_all,
    sums_ss, sums_rs, a2a_ss, k_rs, v_rs, q_rs, fx_ss, fc_ss, fy_ss,
    wz_ss, wz_rs, wr_ss, ws_ss, ws_rs, wx_ss, az_ss, ay_ss, ac_ss, att_rs,
):
    enc_size = lax.axis_size("enc")
    groups = lax.axis_size("head") * enc_size
    rows = q_ref.shape[0]
    inner = lax.axis_size("seq") // groups
    outer = groups
    shares = outer // enc_size
    feature_count = q_ref.shape[1] * groups
    depth, width = w_ref.shape
    pieces = ws_rs.shape[2]
    piece_rows = depth // pieces
    s = lax.axis_index("seq")
    e = lax.axis_index("enc")
    h = lax.axis_index("head")
    g = h * enc_size + e
    a, b = s // inner, s % inner
    other_b, other_e, other_h = 1 - b, 1 - e, 1 - h
    catcher = a % enc_size
    is_catcher = e == catcher
    side = a // 2
    middle = (a + side) % 2
    pending = []

    def plane_of(which_side, is_middle):
        return which_side * (outer - 1) + is_middle * (1 - 2 * which_side)

    def send(src, dst, send_sem, recv_sem, seq_index, group):
        pltpu.make_async_remote_copy(
            src_ref=src, dst_ref=dst, send_sem=send_sem, recv_sem=recv_sem,
            device_id=(seq_index, group // enc_size, group % enc_size),
            device_id_type=pl.DeviceIdType.MESH,
        ).start()

    def wait(ref, sem):
        pltpu.make_async_copy(ref, ref, sem).wait()

    def push(src, dst, send_sem, recv_sem, seq_index, group, when=None):
        pending.append((when, src, send_sem))
        if when is None:
            send(src, dst, send_sem, recv_sem, seq_index, group)
        else:
            @pl.when(when)
            def _():
                send(src, dst, send_sem, recv_sem, seq_index, group)

    def push_or_keep(src, dst, send_sem, recv_sem, seq_index, group, here):
        @pl.when(here)
        def _():
            pltpu.make_async_copy(src, dst, recv_sem).start()

        push(src, dst, send_sem, recv_sem, seq_index, group, jnp.logical_not(here))

    def part_of(p):
        return pl.ds(p * piece_rows, piece_rows)

    def spread(block, origin, slot, p):
        src, dst = block.at[part_of(p)], w_all.at[b, g, part_of(p)]
        push_or_keep(
            src, dst, ws_ss.at[slot, p, 1], ws_rs.at[b, g, p], s, origin, origin == g
        )
        push(
            src, dst, ws_ss.at[slot, p, 0], ws_rs.at[b, g, p], a * inner + other_b, origin,
            None if p % 2 == 0 else origin // enc_size == h,
        )

    def spread_own(p):
        spread(w_ref, a, 0, p)

    def relay(k, p):
        for core in range(enc_size):
            group = other_h * enc_size + core
            piece = w_all.at[b, group, part_of(p)]
            here = g == (a if k is None else arrivals[k])

            @pl.when(here)
            def _():
                wait(piece, ws_rs.at[b, group, p])

            push(
                piece, piece, wx_ss.at[0 if k is None else k + 1, p, core], ws_rs.at[b, group, p],
                a * inner + other_b, g, here,
            )

    near = plane_of(side, 1 - middle)
    far_middle = plane_of(1 - side, 1)
    far_end = plane_of(1 - side, 0)
    own_end = plane_of(side, 0)

    def w_send(k, p):
        push(
            w_ref.at[part_of(p)], w_line.at[a, part_of(p)], wz_ss.at[k, p], wz_rs.at[a, p],
            (far_middle, near)[k] * inner + b, g,
        )

    arrivals = [
        jnp.where(middle == 1, far_middle, near),
        jnp.where(middle == 1, far_end, far_middle),
        jnp.where(middle == 1, near, far_end),
    ]

    def take(k, p):
        origin = arrivals[k]
        piece = w_line.at[origin, part_of(p)]
        wait(piece, wz_rs.at[origin, p])
        if k < 2:
            push(
                piece, piece, wr_ss.at[k, p], wz_rs.at[origin, p],
                own_end * inner + b, g, middle == 1,
            )
        spread(w_line.at[origin], origin, 1 + k, p)

    def share_of(turn):
        return (a // enc_size + turn) % shares

    def block_at(turn, core, column):
        return (share_of(turn) * enc_size + core) * inner + column

    stores = ((v_all, v_rs), (k_all, k_rs))

    def pass_on(kind, turn):
        store, store_rs = stores[kind]
        block = block_at(turn, e, b)
        wait(store.at[block], store_rs.at[block])
        push(
            store.at[block], store.at[block], fx_ss.at[kind, turn], store_rs.at[block],
            a * inner + other_b, g,
        )
        push(
            store.at[block], store.at[block], fc_ss.at[kind, turn], store_rs.at[block],
            s, h * enc_size + other_e,
        )

    def pass_across(kind, turn):
        store, store_rs = stores[kind]
        block = block_at(turn, e, other_b)
        wait(store.at[block], store_rs.at[block])
        push(
            store.at[block], store.at[block], fy_ss.at[kind, turn], store_rs.at[block],
            s, h * enc_size + other_e,
        )

    def gather_rest():
        for store, store_rs in stores:
            for turn in range(shares):
                for column in range(inner):
                    block = block_at(turn, other_e, column)
                    wait(store.at[block], store_rs.at[block])

    key_count = lax.axis_size("seq") * rows

    def attend(turn):
        share = share_of(turn + 1)
        plane = share * enc_size + e
        wait(q_all.at[share], q_rs.at[share])
        scores = lax.dot_general(
            q_all[share], k_all[...].reshape(key_count, HEAD_DIM), (((1,), (1,)), ((), ())),
            preferred_element_type=jnp.float32,
        ) * HEAD_DIM ** (-0.5)
        position = lax.broadcasted_iota(jnp.int32, scores.shape, 1)
        masked = jnp.where(position < limit_ref[0], scores, lowest_score)
        weights = jnp.exp(masked - jnp.max(masked, axis=1, keepdims=True))
        mass = jnp.sum(weights, axis=1, keepdims=True)
        mixed = jnp.dot(
            weights.astype(jnp.bfloat16), v_all[...].reshape(key_count, HEAD_DIM),
            preferred_element_type=jnp.float32,
        )
        att_out[turn] = (mixed / mass).astype(jnp.bfloat16)
        push_or_keep(
            att_out.at[turn], att_all.at[h, a], az_ss.at[turn], att_rs.at[h, a],
            plane * inner + b, g, plane == a,
        )

    def attended_on(ra):
        plane = (a + ra) % outer

        @pl.when(is_catcher)
        def _():
            wait(att_all.at[h, plane], att_rs.at[h, plane])

        push(
            att_all.at[h, plane], att_all.at[h, plane], ay_ss.at[ra], att_rs.at[h, plane],
            s, other_h * enc_size + e, is_catcher,
        )
        push(
            att_all.at[h, plane], att_all.at[h, plane], ac_ss.at[0, ra], att_rs.at[h, plane],
            s, h * enc_size + other_e, is_catcher,
        )

    def attended_across(ra):
        plane = (a + ra) % outer

        @pl.when(is_catcher)
        def _():
            wait(att_all.at[other_h, plane], att_rs.at[other_h, plane])

        push(
            att_all.at[other_h, plane], att_all.at[other_h, plane], ac_ss.at[1, ra],
            att_rs.at[other_h, plane], s, h * enc_size + other_e, is_catcher,
        )

    def attended_rest():
        @pl.when(jnp.logical_not(is_catcher))
        def _():
            for head in range(groups // enc_size):
                for plane in range(outer):
                    wait(att_all.at[head, plane], att_rs.at[head, plane])

    barrier = pltpu.get_barrier_semaphore()
    peers = []
    for ra in range(1, outer):
        for re in range(enc_size):
            peers.append((((a + ra) % outer) * inner + b, h * enc_size + re))
    for rb in range(inner):
        for r in range(groups):
            if rb or r:
                peers.append((a * inner + (b + rb) % inner, (g + r) % groups))
    for seq_index, group in peers:
        pl.semaphore_signal(
            barrier, inc=1, device_id=(seq_index, group // enc_size, group % enc_size),
            device_id_type=pl.DeviceIdType.MESH,
        )

    loads = [
        pltpu.make_async_copy(src, dst, in_sems.at[i])
        for i, (src, dst) in enumerate((
            (q_hbm, q_ref), (k_hbm, k_ref), (v_hbm, v_ref), (qg_hbm, qg_ref), (kg_hbm, kg_ref),
            (limit_hbm, limit_ref), (gate_hbm, gate_ref), (w_hbm, w_ref),
        ))
    ]
    for load in loads:
        load.start()

    ones = jnp.ones((8, 2 * q_ref.shape[1]), jnp.bfloat16)

    def row_sums(ref):
        value = ref[...].astype(jnp.float32)
        square = value * value
        high = square.astype(jnp.bfloat16)
        low = (square - high.astype(jnp.float32)).astype(jnp.bfloat16)
        return lax.dot_general(
            ones, jnp.concatenate([high, low], axis=1), (((1,), (1,)), ((), ())),
            preferred_element_type=jnp.float32,
        )

    loads[0].wait()
    sums[g, 0:8, :] = row_sums(q_ref)
    loads[1].wait()
    sums[g, 8:16, :] = row_sums(k_ref)
    for load in loads[2:]:
        load.wait()
    pl.semaphore_wait(barrier, len(peers))

    for r in range(1, groups):
        push(sums.at[g], sums.at[g], sums_ss.at[r], sums_rs.at[g], s, (g + r) % groups)

    def exchange(kind, i, src, dst, recv_sem):
        plane = e * 2 + i
        push_or_keep(
            src, dst, a2a_ss.at[kind, i], recv_sem, plane * inner + b, h * enc_size + catcher,
            jnp.logical_and(plane == a, is_catcher),
        )

    def send_values():
        for i in range(2):
            exchange(0, i, v_ref.at[:, pl.ds(i * HEAD_DIM, HEAD_DIM)], v_all.at[s], v_rs.at[s])

    def columns_of(rows_of_factors):
        parts, rest = [], rows_of_factors
        for _ in range(3):
            parts.append(rest.astype(jnp.bfloat16))
            rest = rest - parts[-1].astype(jnp.float32)
        row = lax.broadcasted_iota(jnp.int32, (48, 2 * HEAD_DIM), 0) % 16 // 8
        column = lax.broadcasted_iota(jnp.int32, (48, 2 * HEAD_DIM), 1) // HEAD_DIM
        pick = jnp.where(row == column, 0.125, 0.0).astype(jnp.bfloat16)
        return lax.dot_general(
            jnp.concatenate(parts, axis=0), pick, (((0,), (0,)), ((), ())),
            preferred_element_type=jnp.float32,
        )

    def normed(ref, factor, gain, i):
        columns = slice(i * HEAD_DIM, (i + 1) * HEAD_DIM)
        return (ref[:, columns].astype(jnp.float32) * factor * gain[:, columns]).astype(
            jnp.bfloat16
        )

    def send_normed():
        for r in range(1, groups):
            peer = (g + r) % groups
            wait(sums.at[peer], sums_rs.at[peer])
        total = sums[0]
        for r in range(1, groups):
            total = total + sums[r]
        factors = columns_of(lax.rsqrt(total / feature_count + epsilon))
        for i in range(2):
            k_out[i] = normed(k_ref, factors[:, HEAD_DIM:], kg_ref, i)
            exchange(1, i, k_out.at[i], k_all.at[s], k_rs.at[s])
        for i in range(2):
            q_out[i] = normed(q_ref, factors[:, :HEAD_DIM], qg_ref, i)

    def send_queries():
        for i in range(2):
            exchange(2, i, q_out.at[i], q_all.at[a // enc_size], q_rs.at[a // enc_size])

    send_values()
    for p in range(0, 1):
        w_send(1, p)
    for p in range(0, 1):
        w_send(0, p)
    for p in range(0, 1):
        spread_own(p)
    for p in range(1, 2):
        spread_own(p)
    pass_on(0, 0)
    send_normed()
    for p in range(0, 1):
        take(0, p)
    pass_on(1, 0)
    for p in range(1, 2):
        w_send(1, p)
    for p in range(2, 3):
        spread_own(p)
    for p in range(2, 3):
        w_send(1, p)
    for p in range(0, 1):
        take(1, p)
    for p in range(1, 2):
        w_send(0, p)
    pass_on(1, 1)
    for p in range(0, 1):
        take(2, p)
    for p in range(2, 3):
        w_send(0, p)
    pass_across(1, 0)
    pass_on(0, 1)
    for p in range(1, 2):
        take(0, p)
    send_queries()
    for p in range(1, 2):
        take(1, p)
    pass_across(1, 1)
    for p in range(2, 3):
        take(0, p)
    for p in range(1, 2):
        take(2, p)
    pass_across(0, 0)
    pass_across(0, 1)
    for p in range(3, 4):
        spread_own(p)
    for p in range(3, 4):
        w_send(0, p)
    for p in range(2, 3):
        take(1, p)
    relay(1, 1)
    for p in range(3, 4):
        w_send(1, p)
    gather_rest()
    for p in range(2, 3):
        take(2, p)
    attend(0)
    for p in range(3, 4):
        take(0, p)
    relay(None, 3)
    relay(None, 1)
    attend(1)
    relay(0, 1)
    attended_on(0)
    for p in range(3, 4):
        take(1, p)
    relay(2, 1)
    attended_on(1)
    relay(0, 3)
    for p in range(3, 4):
        take(2, p)
    attended_on(2)
    attended_on(3)
    attended_across(0)
    relay(1, 3)
    relay(2, 3)
    attended_across(1)
    attended_across(2)
    attended_across(3)
    attended_rest()

    for turn in range(inner):
        column = (b + turn) % inner
        summed = None
        for group in range(groups):
            for p in range(pieces):
                part = pl.ds(p * piece_rows, piece_rows)
                if p % 2 == 0:
                    wait(w_all.at[column, group, part], ws_rs.at[column, group, p])
                else:
                    @pl.when(jnp.logical_not(jnp.logical_and(column == b, group // enc_size != h)))
                    def _():
                        wait(w_all.at[column, group, part], ws_rs.at[column, group, p])
            head, first = group // enc_size, (group % enc_size) * 2
            lhs = jnp.concatenate([att_all[head, first], att_all[head, first + 1]], axis=1)
            term = jnp.dot(lhs, w_all[column, group], preferred_element_type=jnp.float32)
            term = term.astype(jnp.bfloat16).astype(jnp.float32)
            summed = term if summed is None else summed + term
        columns = pl.ds(pl.multiple_of(column * width, HEAD_DIM), width)
        gates = jnp.where(column == 0, gate_ref[:width][None, :], gate_ref[width:][None, :])
        out_ref[:, columns] = (gates * summed).astype(jnp.bfloat16)

    for when, ref, sem in pending:
        if when is None:
            wait(ref, sem)
        else:
            @pl.when(when)
            def _():
                wait(ref, sem)


def fused(queries, keys, values, out_weight, q_gain, k_gain, gate, valid_count):
    seq_size = lax.axis_size("seq")
    enc_size = lax.axis_size("enc")
    heads = lax.axis_size("head")
    groups = heads * enc_size
    inner = seq_size // groups
    outer = groups
    rows = queries.shape[0]
    depth, width = out_weight.shape
    shares = outer // enc_size
    pieces = 4
    bf16, f32 = jnp.bfloat16, jnp.float32
    dma = pltpu.SemaphoreType.DMA
    hbm = pl.BlockSpec(memory_space=pl.ANY)
    return pl.pallas_call(
        fused_kernel,
        out_shape=pltpu.VMEM((rows, width * inner), bf16),
        in_specs=[hbm] * 8,
        out_specs=pl.BlockSpec(memory_space=pltpu.VMEM),
        scratch_shapes=[
            pltpu.SMEM((1,), jnp.int32),
            pltpu.VMEM(queries.shape, bf16),
            pltpu.VMEM(queries.shape, bf16),
            pltpu.VMEM(queries.shape, bf16),
            pltpu.VMEM((1, queries.shape[1]), f32),
            pltpu.VMEM((1, queries.shape[1]), f32),
            pltpu.VMEM((width * inner,), f32),
            pltpu.VMEM((depth, width), bf16),
            dma((8,)),
            pltpu.VMEM((groups, 16, rows), f32),
            pltpu.VMEM((2, rows, HEAD_DIM), bf16),
            pltpu.VMEM((2, rows, HEAD_DIM), bf16),
            pltpu.VMEM((seq_size, rows, HEAD_DIM), bf16),
            pltpu.VMEM((seq_size, rows, HEAD_DIM), bf16),
            pltpu.VMEM((shares, rows, HEAD_DIM), bf16),
            pltpu.VMEM((outer, depth, width), bf16),
            pltpu.VMEM((inner, groups, depth, width), bf16),
            pltpu.VMEM((shares, rows, HEAD_DIM), bf16),
            pltpu.VMEM((heads, outer, rows, HEAD_DIM), bf16),
            dma((groups,)), dma((groups,)),
            dma((3, 2)), dma((seq_size,)), dma((seq_size,)), dma((shares,)),
            dma((2, shares)), dma((2, shares)), dma((2, shares)),
            dma((2, pieces)), dma((outer, pieces)), dma((2, pieces)),
            dma((outer, pieces, 2)), dma((inner, groups, pieces)),
            dma((outer, pieces, enc_size)),
            dma((shares,)), dma((outer,)), dma((2, outer)), dma((heads, outer)),
        ],
        compiler_params=pltpu.CompilerParams(
            collective_id=0, has_side_effects=True, vmem_limit_bytes=56 * 2**20
        ),
    )(
        valid_count, queries, keys, values, out_weight,
        q_gain[None, :], k_gain[None, :], gate,
    )


def one_kernel_fits(mesh, queries, out_weight):
    sizes = mesh.shape
    seq_size, groups = sizes["seq"], sizes["head"] * sizes["enc"]
    return (
        sizes["enc"] == 2
        and sizes["head"] == 2
        and seq_size == 2 * groups
        and queries.shape[1] == 2 * groups * HEAD_DIM
        and (out_weight.shape[1] // seq_size) % HEAD_DIM == 0
    )


def solution(mesh):
    placed = (
        P("seq", ("head", "enc")),
        P("seq", ("head", "enc")),
        P("seq", ("head", "enc")),
        P(("head", "enc"), "seq"),
        P(("head", "enc")),
        P(("head", "enc")),
        P(("head", "enc")),
        P(),
    )

    def run(*arguments):
        body = fused if one_kernel_fits(mesh, arguments[0], arguments[3]) else local
        return jax.shard_map(
            body, mesh=mesh, in_specs=placed, out_specs=P("seq", ("head", "enc")),
            check_vma=False,
        )(*arguments)

    return run
```

```python
import jax
import jax.numpy as jnp
from jax import lax
from jax.experimental import pallas as pl
from jax.experimental.pallas import tpu as pltpu
from jax.sharding import PartitionSpec as P

HEAD_DIM = 128


epsilon = 1e-06
lowest_score = -1e30


def normalize(matrix, squares, gain_row, feature_count):
    inverse_rms = lax.rsqrt(squares / feature_count + epsilon)
    return (matrix.astype(jnp.float32) * inverse_rms[:, None] * gain_row[None, :]).astype(
        jnp.bfloat16
    )


def absorb(carried, query_heads, key_block, value_block, offset, key_limit):
    running_sum, running_max, running_mass = carried
    scale_factor = query_heads.shape[2] ** (-0.5)
    scores = (
        jnp.einsum("qhd,khd->hqk", query_heads, key_block, preferred_element_type=jnp.float32)
        * scale_factor
    )
    position = offset + jnp.arange(key_block.shape[0], dtype=jnp.int32)
    usable = (position < key_limit)[None, None, :]
    masked = jnp.where(usable, scores, lowest_score)
    new_max = jnp.maximum(running_max, jnp.max(masked, axis=2))
    weights = jnp.where(usable, jnp.exp(masked - new_max[:, :, None]), 0.0)
    factor = jnp.exp(running_max - new_max)
    running_mass = running_mass * factor + jnp.sum(weights, axis=2)
    running_sum = running_sum * factor[:, :, None] + jnp.einsum(
        "hqk,khd->hqd",
        weights.astype(jnp.bfloat16),
        value_block,
        preferred_element_type=jnp.float32,
    )
    return (running_sum, new_max, running_mass)


def absorb_blocks(carried, query_heads, key_rows, value_rows, key_limit):
    row_total = key_rows.shape[0]
    block_size = 512
    block_count = row_total // block_size
    key_blocks = key_rows.reshape((block_count, block_size) + key_rows.shape[1:])
    value_blocks = value_rows.reshape((block_count, block_size) + value_rows.shape[1:])

    def absorb_block(running, triple):
        block_number, key_block, value_block = triple
        return (
            absorb(
                running, query_heads, key_block, value_block, block_number * block_size, key_limit
            ),
            None,
        )

    numbers = jnp.arange(block_count, dtype=jnp.int32)
    carried, _ = lax.scan(absorb_block, carried, (numbers, key_blocks, value_blocks))
    return carried


def visit(carried, query_heads, key_rows, value_rows, offset, key_limit):
    return lax.cond(
        offset < key_limit,
        lambda running: absorb_blocks(running, query_heads, key_rows, value_rows, key_limit),
        lambda running: running,
        carried,
    )


def local(queries, keys, values, out_weight, q_gain, k_gain, gate, valid_count):
    row_count = queries.shape[0]
    local_heads = queries.shape[1] // HEAD_DIM
    feature_count = queries.shape[1] * lax.axis_size(("head", "enc"))
    key_limit = valid_count[0]
    query_squares = jnp.sum(jnp.square(queries.astype(jnp.float32)), axis=1)
    key_squares = jnp.sum(jnp.square(keys.astype(jnp.float32)), axis=1)
    query_totals, key_totals = lax.psum((query_squares, key_squares), ("head", "enc"))
    query_heads = normalize(queries, query_totals, q_gain, feature_count).reshape(
        row_count, local_heads, HEAD_DIM
    )
    key_heads = normalize(keys, key_totals, k_gain, feature_count).reshape(
        row_count, local_heads, HEAD_DIM
    )
    value_heads = values.reshape(row_count, local_heads, HEAD_DIM)
    initial = (
        jnp.zeros((local_heads, row_count, HEAD_DIM), jnp.float32),
        jnp.full((local_heads, row_count), lowest_score, jnp.float32),
        jnp.zeros((local_heads, row_count), jnp.float32),
    )
    running_sum, running_max, running_mass = visit(
        initial,
        query_heads,
        lax.all_gather(key_heads, "seq", axis=0, tiled=True),
        lax.all_gather(value_heads, "seq", axis=0, tiled=True),
        jnp.int32(0),
        key_limit,
    )
    attended = (running_sum / running_mass[:, :, None]).transpose(1, 0, 2)
    attended = attended.reshape(row_count, local_heads * HEAD_DIM).astype(jnp.bfloat16)
    terms = jnp.dot(
        attended,
        lax.all_gather(out_weight, "seq", axis=1, tiled=True),
        preferred_element_type=jnp.float32,
    )
    summed = lax.psum_scatter(
        terms.astype(jnp.bfloat16), ("head", "enc"), scatter_dimension=1, tiled=True
    ).astype(jnp.float32)
    return (gate[None, :] * summed).astype(jnp.bfloat16)


def fused_kernel(
    limit_hbm, q_hbm, k_hbm, v_hbm, w_hbm, qg_hbm, kg_hbm, gate_hbm, out_ref,
    limit_ref, q_ref, k_ref, v_ref, qg_ref, kg_ref, gate_ref, w_ref, in_sems,
    sums, k_out, q_out, k_all, v_all, q_all, w_line, w_all, att_out, att_all,
    sums_ss, sums_rs, a2a_ss, k_rs, v_rs, q_rs, fx_ss, fc_ss, fy_ss,
    wz_ss, wz_rs, wr_ss, ws_ss, ws_rs, wx_ss, az_ss, ay_ss, ac_ss, att_rs,
):
    enc_size = lax.axis_size("enc")
    groups = lax.axis_size("head") * enc_size
    rows = q_ref.shape[0]
    inner = lax.axis_size("seq") // groups
    outer = groups
    shares = outer // enc_size
    feature_count = q_ref.shape[1] * groups
    depth, width = w_ref.shape
    pieces = ws_rs.shape[2]
    piece_rows = depth // pieces
    s = lax.axis_index("seq")
    e = lax.axis_index("enc")
    h = lax.axis_index("head")
    g = h * enc_size + e
    a, b = s // inner, s % inner
    other_b, other_e, other_h = 1 - b, 1 - e, 1 - h
    catcher = a % enc_size
    is_catcher = e == catcher
    side = a // 2
    middle = (a + side) % 2
    pending = []

    def plane_of(which_side, is_middle):
        return which_side * (outer - 1) + is_middle * (1 - 2 * which_side)

    def send(src, dst, send_sem, recv_sem, seq_index, group):
        pltpu.make_async_remote_copy(
            src_ref=src, dst_ref=dst, send_sem=send_sem, recv_sem=recv_sem,
            device_id=(seq_index, group // enc_size, group % enc_size),
            device_id_type=pl.DeviceIdType.MESH,
        ).start()

    def wait(ref, sem):
        pltpu.make_async_copy(ref, ref, sem).wait()

    def push(src, dst, send_sem, recv_sem, seq_index, group, when=None):
        pending.append((when, src, send_sem))
        if when is None:
            send(src, dst, send_sem, recv_sem, seq_index, group)
        else:
            @pl.when(when)
            def _():
                send(src, dst, send_sem, recv_sem, seq_index, group)

    def push_or_keep(src, dst, send_sem, recv_sem, seq_index, group, here):
        @pl.when(here)
        def _():
            pltpu.make_async_copy(src, dst, recv_sem).start()

        push(src, dst, send_sem, recv_sem, seq_index, group, jnp.logical_not(here))

    def part_of(p):
        return pl.ds(p * piece_rows, piece_rows)

    def spread(block, origin, slot, p):
        src, dst = block.at[part_of(p)], w_all.at[b, g, part_of(p)]
        push_or_keep(
            src, dst, ws_ss.at[slot, p, 1], ws_rs.at[b, g, p], s, origin, origin == g
        )
        push(
            src, dst, ws_ss.at[slot, p, 0], ws_rs.at[b, g, p], a * inner + other_b, origin,
            None if p % 2 == 0 else origin // enc_size == h,
        )

    def spread_own(p):
        spread(w_ref, a, 0, p)

    def relay(k, p):
        for core in range(enc_size):
            group = other_h * enc_size + core
            piece = w_all.at[b, group, part_of(p)]
            here = g == (a if k is None else arrivals[k])

            @pl.when(here)
            def _():
                wait(piece, ws_rs.at[b, group, p])

            push(
                piece, piece, wx_ss.at[0 if k is None else k + 1, p, core], ws_rs.at[b, group, p],
                a * inner + other_b, g, here,
            )

    near = plane_of(side, 1 - middle)
    far_middle = plane_of(1 - side, 1)
    far_end = plane_of(1 - side, 0)
    own_end = plane_of(side, 0)

    def w_send(k, p):
        push(
            w_ref.at[part_of(p)], w_line.at[a, part_of(p)], wz_ss.at[k, p], wz_rs.at[a, p],
            (far_middle, near)[k] * inner + b, g,
        )

    arrivals = [
        jnp.where(middle == 1, far_middle, near),
        jnp.where(middle == 1, far_end, far_middle),
        jnp.where(middle == 1, near, far_end),
    ]

    def take(k, p):
        origin = arrivals[k]
        piece = w_line.at[origin, part_of(p)]
        wait(piece, wz_rs.at[origin, p])
        if k < 2:
            push(
                piece, piece, wr_ss.at[k, p], wz_rs.at[origin, p],
                own_end * inner + b, g, middle == 1,
            )
        spread(w_line.at[origin], origin, 1 + k, p)

    def share_of(turn):
        return (a // enc_size + turn) % shares

    def block_at(turn, core, column):
        return (share_of(turn) * enc_size + core) * inner + column

    stores = ((v_all, v_rs), (k_all, k_rs))

    def pass_on(kind, turn):
        store, store_rs = stores[kind]
        block = block_at(turn, e, b)
        wait(store.at[block], store_rs.at[block])
        push(
            store.at[block], store.at[block], fx_ss.at[kind, turn], store_rs.at[block],
            a * inner + other_b, g,
        )
        push(
            store.at[block], store.at[block], fc_ss.at[kind, turn], store_rs.at[block],
            s, h * enc_size + other_e,
        )

    def pass_across(kind, turn):
        store, store_rs = stores[kind]
        block = block_at(turn, e, other_b)
        wait(store.at[block], store_rs.at[block])
        push(
            store.at[block], store.at[block], fy_ss.at[kind, turn], store_rs.at[block],
            s, h * enc_size + other_e,
        )

    def gather_rest():
        for store, store_rs in stores:
            for turn in range(shares):
                for column in range(inner):
                    block = block_at(turn, other_e, column)
                    wait(store.at[block], store_rs.at[block])

    key_count = lax.axis_size("seq") * rows

    def attend(turn):
        share = share_of(turn + 1)
        plane = share * enc_size + e
        wait(q_all.at[share], q_rs.at[share])
        scores = lax.dot_general(
            q_all[share], k_all[...].reshape(key_count, HEAD_DIM), (((1,), (1,)), ((), ())),
            preferred_element_type=jnp.float32,
        ) * HEAD_DIM ** (-0.5)
        position = lax.broadcasted_iota(jnp.int32, scores.shape, 1)
        masked = jnp.where(position < limit_ref[0], scores, lowest_score)
        weights = jnp.exp(masked - jnp.max(masked, axis=1, keepdims=True))
        mass = jnp.sum(weights, axis=1, keepdims=True)
        mixed = jnp.dot(
            weights.astype(jnp.bfloat16), v_all[...].reshape(key_count, HEAD_DIM),
            preferred_element_type=jnp.float32,
        )
        att_out[turn] = (mixed / mass).astype(jnp.bfloat16)
        push_or_keep(
            att_out.at[turn], att_all.at[h, a], az_ss.at[turn], att_rs.at[h, a],
            plane * inner + b, g, plane == a,
        )

    def attended_on(ra):
        plane = (a + ra) % outer

        @pl.when(is_catcher)
        def _():
            wait(att_all.at[h, plane], att_rs.at[h, plane])

        push(
            att_all.at[h, plane], att_all.at[h, plane], ay_ss.at[ra], att_rs.at[h, plane],
            s, other_h * enc_size + e, is_catcher,
        )
        push(
            att_all.at[h, plane], att_all.at[h, plane], ac_ss.at[0, ra], att_rs.at[h, plane],
            s, h * enc_size + other_e, is_catcher,
        )

    def attended_across(ra):
        plane = (a + ra) % outer

        @pl.when(is_catcher)
        def _():
            wait(att_all.at[other_h, plane], att_rs.at[other_h, plane])

        push(
            att_all.at[other_h, plane], att_all.at[other_h, plane], ac_ss.at[1, ra],
            att_rs.at[other_h, plane], s, h * enc_size + other_e, is_catcher,
        )

    def attended_rest():
        @pl.when(jnp.logical_not(is_catcher))
        def _():
            for head in range(groups // enc_size):
                for plane in range(outer):
                    wait(att_all.at[head, plane], att_rs.at[head, plane])

    barrier = pltpu.get_barrier_semaphore()
    peers = []
    for ra in range(1, outer):
        for re in range(enc_size):
            peers.append((((a + ra) % outer) * inner + b, h * enc_size + re))
    for rb in range(inner):
        for r in range(groups):
            if rb or r:
                peers.append((a * inner + (b + rb) % inner, (g + r) % groups))
    for seq_index, group in peers:
        pl.semaphore_signal(
            barrier, inc=1, device_id=(seq_index, group // enc_size, group % enc_size),
            device_id_type=pl.DeviceIdType.MESH,
        )

    loads = [
        pltpu.make_async_copy(src, dst, in_sems.at[i])
        for i, (src, dst) in enumerate((
            (q_hbm, q_ref), (k_hbm, k_ref), (v_hbm, v_ref), (qg_hbm, qg_ref), (kg_hbm, kg_ref),
            (limit_hbm, limit_ref), (gate_hbm, gate_ref), (w_hbm, w_ref),
        ))
    ]
    for load in loads:
        load.start()

    ones = jnp.ones((8, 2 * q_ref.shape[1]), jnp.bfloat16)

    def row_sums(ref):
        value = ref[...].astype(jnp.float32)
        square = value * value
        high = square.astype(jnp.bfloat16)
        low = (square - high.astype(jnp.float32)).astype(jnp.bfloat16)
        return lax.dot_general(
            ones, jnp.concatenate([high, low], axis=1), (((1,), (1,)), ((), ())),
            preferred_element_type=jnp.float32,
        )

    loads[0].wait()
    sums[g, 0:8, :] = row_sums(q_ref)
    loads[1].wait()
    sums[g, 8:16, :] = row_sums(k_ref)
    for load in loads[2:]:
        load.wait()
    pl.semaphore_wait(barrier, len(peers))

    for r in range(1, groups):
        push(sums.at[g], sums.at[g], sums_ss.at[r], sums_rs.at[g], s, (g + r) % groups)

    def exchange(kind, i, src, dst, recv_sem):
        plane = e * 2 + i
        push_or_keep(
            src, dst, a2a_ss.at[kind, i], recv_sem, plane * inner + b, h * enc_size + catcher,
            jnp.logical_and(plane == a, is_catcher),
        )

    def send_values():
        for i in range(2):
            exchange(0, i, v_ref.at[:, pl.ds(i * HEAD_DIM, HEAD_DIM)], v_all.at[s], v_rs.at[s])

    def columns_of(rows_of_factors):
        parts, rest = [], rows_of_factors
        for _ in range(3):
            parts.append(rest.astype(jnp.bfloat16))
            rest = rest - parts[-1].astype(jnp.float32)
        row = lax.broadcasted_iota(jnp.int32, (48, 2 * HEAD_DIM), 0) % 16 // 8
        column = lax.broadcasted_iota(jnp.int32, (48, 2 * HEAD_DIM), 1) // HEAD_DIM
        pick = jnp.where(row == column, 0.125, 0.0).astype(jnp.bfloat16)
        return lax.dot_general(
            jnp.concatenate(parts, axis=0), pick, (((0,), (0,)), ((), ())),
            preferred_element_type=jnp.float32,
        )

    def normed(ref, factor, gain, i):
        columns = slice(i * HEAD_DIM, (i + 1) * HEAD_DIM)
        return (ref[:, columns].astype(jnp.float32) * factor * gain[:, columns]).astype(
            jnp.bfloat16
        )

    def send_normed():
        for r in range(1, groups):
            peer = (g + r) % groups
            wait(sums.at[peer], sums_rs.at[peer])
        total = sums[0]
        for r in range(1, groups):
            total = total + sums[r]
        factors = columns_of(lax.rsqrt(total / feature_count + epsilon))
        for i in range(2):
            k_out[i] = normed(k_ref, factors[:, HEAD_DIM:], kg_ref, i)
            exchange(1, i, k_out.at[i], k_all.at[s], k_rs.at[s])
        for i in range(2):
            q_out[i] = normed(q_ref, factors[:, :HEAD_DIM], qg_ref, i)

    def send_queries():
        for i in range(2):
            exchange(2, i, q_out.at[i], q_all.at[a // enc_size], q_rs.at[a // enc_size])

    send_values()
    for p in range(0, 1):
        w_send(1, p)
    for p in range(0, 1):
        w_send(0, p)
    for p in range(0, 1):
        spread_own(p)
    for p in range(1, 2):
        spread_own(p)
    pass_on(0, 0)
    send_normed()
    for p in range(0, 1):
        take(0, p)
    pass_on(1, 0)
    for p in range(1, 2):
        w_send(1, p)
    for p in range(2, 3):
        spread_own(p)
    for p in range(2, 3):
        w_send(1, p)
    for p in range(0, 1):
        take(1, p)
    for p in range(1, 2):
        w_send(0, p)
    pass_on(1, 1)
    for p in range(0, 1):
        take(2, p)
    for p in range(2, 3):
        w_send(0, p)
    pass_across(1, 0)
    pass_on(0, 1)
    for p in range(1, 2):
        take(0, p)
    send_queries()
    for p in range(1, 2):
        take(1, p)
    pass_across(1, 1)
    for p in range(2, 3):
        take(0, p)
    for p in range(1, 2):
        take(2, p)
    pass_across(0, 0)
    pass_across(0, 1)
    for p in range(3, 4):
        spread_own(p)
    for p in range(3, 4):
        w_send(0, p)
    for p in range(2, 3):
        take(1, p)
    relay(1, 1)
    for p in range(3, 4):
        w_send(1, p)
    gather_rest()
    for p in range(2, 3):
        take(2, p)
    attend(0)
    for p in range(3, 4):
        take(0, p)
    relay(None, 3)
    relay(None, 1)
    attend(1)
    relay(0, 1)
    attended_on(0)
    for p in range(3, 4):
        take(1, p)
    relay(2, 1)
    attended_on(1)
    relay(0, 3)
    for p in range(3, 4):
        take(2, p)
    attended_on(2)
    attended_on(3)
    attended_across(0)
    relay(1, 3)
    relay(2, 3)
    attended_across(1)
    attended_across(2)
    attended_across(3)
    attended_rest()

    for turn in range(inner):
        column = (b + turn) % inner
        summed = None
        for step in range(groups):
            across, first = step // enc_size, (step % enc_size) * 2
            head = (h + across) % (groups // enc_size)
            group = head * enc_size + step % enc_size
            for p in range(pieces):
                part = pl.ds(p * piece_rows, piece_rows)
                if p % 2 == 0 or turn or not across:
                    wait(w_all.at[column, group, part], ws_rs.at[column, group, p])
            lhs = jnp.concatenate([att_all[head, first], att_all[head, first + 1]], axis=1)
            term = jnp.dot(lhs, w_all[column, group], preferred_element_type=jnp.float32)
            term = term.astype(jnp.bfloat16).astype(jnp.float32)
            summed = term if summed is None else summed + term
        columns = pl.ds(pl.multiple_of(column * width, HEAD_DIM), width)
        gates = jnp.where(column == 0, gate_ref[:width][None, :], gate_ref[width:][None, :])
        out_ref[:, columns] = (gates * summed).astype(jnp.bfloat16)

    for when, ref, sem in pending:
        if when is None:
            wait(ref, sem)
        else:
            @pl.when(when)
            def _():
                wait(ref, sem)


def fused(queries, keys, values, out_weight, q_gain, k_gain, gate, valid_count):
    seq_size = lax.axis_size("seq")
    enc_size = lax.axis_size("enc")
    heads = lax.axis_size("head")
    groups = heads * enc_size
    inner = seq_size // groups
    outer = groups
    rows = queries.shape[0]
    depth, width = out_weight.shape
    shares = outer // enc_size
    pieces = 4
    bf16, f32 = jnp.bfloat16, jnp.float32
    dma = pltpu.SemaphoreType.DMA
    hbm = pl.BlockSpec(memory_space=pl.ANY)
    return pl.pallas_call(
        fused_kernel,
        out_shape=pltpu.VMEM((rows, width * inner), bf16),
        in_specs=[hbm] * 8,
        out_specs=pl.BlockSpec(memory_space=pltpu.VMEM),
        scratch_shapes=[
            pltpu.SMEM((1,), jnp.int32),
            pltpu.VMEM(queries.shape, bf16),
            pltpu.VMEM(queries.shape, bf16),
            pltpu.VMEM(queries.shape, bf16),
            pltpu.VMEM((1, queries.shape[1]), f32),
            pltpu.VMEM((1, queries.shape[1]), f32),
            pltpu.VMEM((width * inner,), f32),
            pltpu.VMEM((depth, width), bf16),
            dma((8,)),
            pltpu.VMEM((groups, 16, rows), f32),
            pltpu.VMEM((2, rows, HEAD_DIM), bf16),
            pltpu.VMEM((2, rows, HEAD_DIM), bf16),
            pltpu.VMEM((seq_size, rows, HEAD_DIM), bf16),
            pltpu.VMEM((seq_size, rows, HEAD_DIM), bf16),
            pltpu.VMEM((shares, rows, HEAD_DIM), bf16),
            pltpu.VMEM((outer, depth, width), bf16),
            pltpu.VMEM((inner, groups, depth, width), bf16),
            pltpu.VMEM((shares, rows, HEAD_DIM), bf16),
            pltpu.VMEM((heads, outer, rows, HEAD_DIM), bf16),
            dma((groups,)), dma((groups,)),
            dma((3, 2)), dma((seq_size,)), dma((seq_size,)), dma((shares,)),
            dma((2, shares)), dma((2, shares)), dma((2, shares)),
            dma((2, pieces)), dma((outer, pieces)), dma((2, pieces)),
            dma((outer, pieces, 2)), dma((inner, groups, pieces)),
            dma((outer, pieces, enc_size)),
            dma((shares,)), dma((outer,)), dma((2, outer)), dma((heads, outer)),
        ],
        compiler_params=pltpu.CompilerParams(
            collective_id=0, has_side_effects=True, vmem_limit_bytes=56 * 2**20
        ),
    )(
        valid_count, queries, keys, values, out_weight,
        q_gain[None, :], k_gain[None, :], gate,
    )


def one_kernel_fits(mesh, queries, out_weight):
    sizes = mesh.shape
    seq_size, groups = sizes["seq"], sizes["head"] * sizes["enc"]
    return (
        sizes["enc"] == 2
        and sizes["head"] == 2
        and seq_size == 2 * groups
        and queries.shape[1] == 2 * groups * HEAD_DIM
        and (out_weight.shape[1] // seq_size) % HEAD_DIM == 0
    )


def solution(mesh):
    placed = (
        P("seq", ("head", "enc")),
        P("seq", ("head", "enc")),
        P("seq", ("head", "enc")),
        P(("head", "enc"), "seq"),
        P(("head", "enc")),
        P(("head", "enc")),
        P(("head", "enc")),
        P(),
    )

    def run(*arguments):
        body = fused if one_kernel_fits(mesh, arguments[0], arguments[3]) else local
        return jax.shard_map(
            body, mesh=mesh, in_specs=placed, out_specs=P("seq", ("head", "enc")),
            check_vma=False,
        )(*arguments)

    return run
```
